128 devices in a mesh: freq: 4 (over x_hi, core), sky: 32 (over x_lo, y, z).
Axes of the slice: x: 4 (x_hi: 2, x_lo: 2; x = x_hi * 2 + x_lo), y: 4, z: 4, core: 2. Of those that a mesh axis runs over, the one named last changes fastest.
Arguments:
- sky_cube: bfloat16 [16, 1024, 1024], P('freq', 'sky'), may hold values from -6 to 6
- half_width: int32 [16], P('freq'), may hold values from 2 to 12, as said below
- conv_weight: bfloat16 [16, 27], replicated, may hold values from -0.3125 to 0.3125
- out_cotangent: bfloat16 [16, 16, 1024, 1024], P(None, 'freq', 'sky'), may hold values from -6 to 6
Outputs:
- sky_grad: float32 [16, 1024, 1024], P('freq', 'sky')
- kernel_grad: float32 [16, 27], replicated
The draws below stay inside these ranges and needn't reach their ends.
Inputs may be any that keep to these rules, and one draw needn't show every extreme that they name: half_width[f] differs by at most one from 2 + floor((10) (15 - f) / 15); the first frequency has exactly 12 and the last exactly 2.
All inputs are finite; a program needn't handle non-finite values.
Results may differ from the reference program's by a relative error of at most 0.0033.
Values may be sent and summed in bfloat16 or wider, within the bound.
No kernel may reach another device: no remote copies, remote signals or barrier semaphores. Data moves between devices by JAX's collectives and lax.ppermute only.
A program may use at most 128 MiB of HBM per device.

```python
import math
import jax
import jax.numpy as jnp
from jax import lax

V = 1024
CH = 16
TAPS = 27
MAXH = 12
FREQS = 16
U = 1024


def draw_half_width(key, part):
    freq_index = jnp.arange(FREQS, dtype=jnp.int32)
    base_width = 2 + (MAXH - 2) * (FREQS - 1 - freq_index) // (FREQS - 1)
    jitter = jax.random.randint(key, (FREQS,), -1, 2, dtype=jnp.int32)
    widths = jnp.clip(base_width + jitter, 2, MAXH)
    widths = widths.at[0].set(MAXH).at[FREQS - 1].set(2)
    return widths.astype(jnp.int32)


def block_levels(key, shape, cuts, low, largest):
    factor_of = 1.0
    for position, shards_of in cuts:
        draws = jax.random.uniform(jax.random.fold_in(jax.random.fold_in(key, 6), position), (shards_of,), jnp.float32, low / len(cuts), largest / len(cuts))
        factor_of = factor_of * jnp.repeat(jnp.exp(draws), shape[position] // shards_of).reshape((-1,) + (1,) * (len(shape) - 1 - position))
    return factor_of


def gaussian(rng, dims, width, bound, pieces=(), held_as=jnp.bfloat16):
    array = width * jax.random.normal(rng, dims, jnp.float32)
    if pieces:
        array = array * block_levels(rng, dims, pieces, -0.22, 0.18)
    return jnp.clip(array, -bound, bound).astype(held_as)


def setup_inputs(seed: int = 0) -> dict:
    splits = jax.random.split(jax.random.key(seed), 5)
    return {
        "sky_cube": gaussian(splits[0], (FREQS, U, V), 1.0, 6.0, ((0, 4), (1, 32))),
        "half_width": draw_half_width(jax.random.fold_in(splits[4], 71), 0),
        "conv_weight": gaussian(splits[2], (CH, TAPS), (CH * TAPS) ** -0.5, 0.3125),
        "out_cotangent": gaussian(splits[3], (CH, FREQS, U, V), 1.0, 6.0, ((1, 4), (2, 32))),
    }


def beam_taps(half_width):
    offsets = jnp.arange(-MAXH, MAXH + 1, dtype=jnp.int32)
    inside = jnp.abs(offsets)[None, :] <= half_width[:, None]
    spread = half_width.astype(jnp.float32)[:, None]
    offset_sq = (offsets.astype(jnp.float32) ** 2)[None, :]
    profile = jnp.where(inside, jnp.exp(-2.0 * offset_sq / (spread * spread)), jnp.float32(0.0))
    return profile / jnp.sqrt(lax.optimization_barrier(jnp.sum(profile * profile, axis=1, keepdims=True)))

def blur_columns(source, kernel_taps):
    length = source.shape[2]
    padded = jnp.pad(source, ((0, 0), (0, 0), (MAXH, MAXH)))
    summed = jnp.zeros_like(source)
    for j in range(2 * MAXH + 1):
        summed = summed + kernel_taps[:, j][:, None, None] * padded[:, :, j:j + length]
    return summed

def blur_rows(source, kernel_taps):
    length = source.shape[1]
    padded = jnp.pad(source, ((0, 0), (MAXH, MAXH), (0, 0)))
    summed = jnp.zeros_like(source)
    for j in range(2 * MAXH + 1):
        summed = summed + kernel_taps[:, j][:, None, None] * padded[:, j:j + length, :]
    return summed

def reference(sky_cube, half_width, conv_weight, out_cotangent):
    kernel_taps = beam_taps(half_width)
    beam_field = blur_rows(blur_columns(sky_cube.astype(jnp.float32), kernel_taps), kernel_taps).astype(jnp.bfloat16)
    framed = jnp.pad(beam_field, 1)
    cot_pad = jnp.pad(out_cotangent, ((0, 0), (1, 1), (1, 1), (1, 1)))
    weights = conv_weight.astype(jnp.float32)
    row_count = beam_field.shape[1]
    col_count = beam_field.shape[2]

    def plane_terms(plane_index):
        cot_plane = lax.dynamic_index_in_dim(out_cotangent, plane_index, 1, keepdims=False).astype(jnp.float32)
        beam_block = lax.dynamic_slice_in_dim(framed, plane_index, 3, 0).astype(jnp.float32)
        cot_block = lax.dynamic_slice_in_dim(cot_pad, plane_index, 3, 1).astype(jnp.float32)
        grad_terms = []
        back_plane = jnp.zeros((row_count, col_count), jnp.float32)
        for a in range(3):
            for b in range(3):
                for e in range(3):
                    shifted = beam_block[a, b:b + row_count, e:e + col_count]
                    grad_terms.append(jnp.einsum('cuv,uv->c', cot_plane, shifted))
                    moved = cot_block[:, 2 - a, 2 - b:2 - b + row_count, 2 - e:2 - e + col_count]
                    back_plane = back_plane + jnp.einsum('c,cuv->uv', weights[:, 9 * a + 3 * b + e], moved)
        return (jnp.stack(grad_terms, axis=1), back_plane)
    grad_terms, back_planes = lax.map(plane_terms, jnp.arange(beam_field.shape[0], dtype=jnp.int32))
    kernel_grad = lax.optimization_barrier(jnp.sum(grad_terms, axis=0)) * (1.0 / math.sqrt(FREQS * U * V))
    grad_beam = back_planes.astype(jnp.bfloat16)
    sky_grad = blur_rows(blur_columns(grad_beam.astype(jnp.float32), kernel_taps), kernel_taps)
    return (sky_grad, kernel_grad)
```

```python
import math

import jax
import jax.numpy as jnp
from jax import lax
from jax.experimental import pallas as pl
from jax.experimental.pallas import tpu as pltpu
from jax.sharding import PartitionSpec as P

MAXH = 12
HALF = 16
F32 = jnp.float32
BF16 = jnp.bfloat16
VMEM_LIMIT = 48 * 1024 * 1024


def params():
    return pltpu.CompilerParams(vmem_limit_bytes=VMEM_LIMIT)


def iota(shape, dim):
    return lax.broadcasted_iota(jnp.int32, shape, dim)


def dot(a, b):
    return jnp.dot(a, b, preferred_element_type=F32)


def split(x):
    hi = x.astype(BF16)
    return hi, (x - hi.astype(F32)).astype(BF16)


def taps_at(offsets, width):
    def profile(d):
        w = jnp.full(d.shape, width, jnp.int32)
        wf = w.astype(F32)
        df = d.astype(F32)
        return jnp.where(jnp.abs(d) <= w, jnp.exp(-2.0 * (df * df) / (wf * wf)), 0.0)

    line = profile(iota((8, 128), 1) - 64)
    norm = jnp.sqrt(jnp.sum(line * line, axis=1, keepdims=True))[:1]
    return profile(offsets) / norm


def column_matrices(width):
    band = taps_at(iota((160, 128), 0) - 16 - iota((160, 128), 1), width)
    left = jnp.concatenate([jnp.zeros((112, 128), F32), band, jnp.zeros((240, 128), F32)], axis=0)
    right = jnp.concatenate([jnp.zeros((240, 128), F32), band, jnp.zeros((112, 128), F32)], axis=0)
    return split(jnp.concatenate([left, right], axis=1))


def blur_columns(rows, width):
    n = rows.shape[0]
    hi, lo = column_matrices(width)
    edge = jnp.zeros((n, 128), BF16)
    padded = jnp.concatenate([edge, rows, edge], axis=1)
    stacked = jnp.concatenate([padded[:, 256 * j : 256 * j + 512] for j in range(4)], axis=0)
    out = dot(stacked, hi) + dot(stacked, lo)
    return jnp.concatenate([out[n * j : n * j + n] for j in range(4)], axis=1)


def blur_rows(source, count, base, width):
    n = source.shape[0]
    matrix = taps_at(iota((count, n), 1) - iota((count, n), 0) - base, width)
    m_hi, m_lo = split(matrix)
    hi, lo = split(source)
    return dot(m_hi, hi) + dot(m_hi, lo) + dot(m_lo, hi)


def shift_cols(x, offset):
    if offset == 0:
        return x
    length = x.shape[-1]
    col = iota(x.shape, x.ndim - 1)
    if offset > 0:
        return jnp.where(col < length - 1, pltpu.roll(x, length - 1, x.ndim - 1), 0.0)
    return jnp.where(col > 0, pltpu.roll(x, 1, x.ndim - 1), 0.0)


def back_kernel(weight_ref, cot_ref, out_ref, mat_ref, acc_ref):
    f = pl.program_id(0)

    @pl.when(f == 0)
    def _():
        expand = (iota((16, 512), 1) // 32 == iota((16, 512), 0)).astype(BF16)
        w = lax.dot_general(weight_ref[...], expand, (((0,), (0,)), ((), ())), preferred_element_type=F32)
        diff = iota((40, 512), 0) - iota((40, 512), 1) % 32
        blocks = []
        for a in range(3):
            for e in range(3):
                block = jnp.zeros((40, 512), F32)
                for b in range(3):
                    row = w[9 * a + 3 * b + e : 9 * a + 3 * b + e + 1, :]
                    block = jnp.where(diff == b, row, block)
                blocks.append(block)
        mat_ref[...] = jnp.concatenate(blocks, axis=0).astype(BF16)
        acc_ref[...] = jnp.zeros_like(acc_ref)

    cot = cot_ref[...].reshape(512, 1024)
    terms = dot(mat_ref[...], cot)
    for a in range(3):
        acc_ref[pl.ds(f + a, 1)] += terms[120 * a : 120 * a + 120][None]

    @pl.when(f == pl.num_programs(0) - 1)
    def _():
        for p in range(6):
            full = acc_ref[p]
            out_ref[p] = shift_cols(full[0:40], 1) + full[40:80] + shift_cols(full[80:120], -1)


def back_project(conv_weight, out_cotangent):
    return pl.pallas_call(
        back_kernel,
        grid=(4,),
        out_shape=jax.ShapeDtypeStruct((6, 40, 1024), F32),
        in_specs=[
            pl.BlockSpec((16, 27), lambda f: (0, 0)),
            pl.BlockSpec((16, 1, 32, 1024), lambda f: (0, f, 0, 0)),
        ],
        out_specs=pl.BlockSpec((6, 40, 1024), lambda f: (0, 0, 0)),
        scratch_shapes=[pltpu.VMEM((360, 512), BF16), pltpu.VMEM((6, 120, 1024), F32)],
        compiler_params=params(),
        cost_estimate=pl.CostEstimate(flops=3 * 10**9, bytes_accessed=6 * 2**20, transcendentals=0),
        name="back_project",
    )(conv_weight, out_cotangent)


def beam_kernel(where_ref, width_ref, sky_ref, a_ref, b_ref, beam_ref):
    even = where_ref[0] % 2 == 0
    row = iota((48, 1024), 0)
    first = jnp.where(where_ref[0] == 0, 1, 0)
    last = jnp.where(where_ref[0] == 31, 33, 34)
    keep = (row >= first) & (row < last)
    for f in range(4):
        width = width_ref[f]
        ra, rb = a_ref[f], b_ref[f]
        above = jnp.where(even, rb, ra)
        below = jnp.where(even, ra, rb)
        rows = jnp.concatenate([above, sky_ref[f], below], axis=0)
        smooth = blur_columns(rows, width)
        beam = jnp.where(keep, blur_rows(smooth, 48, 15, width), 0.0)
        beam_ref[f] = beam.astype(BF16)


def smem():
    return pl.BlockSpec(memory_space=pltpu.SMEM)


def vmem():
    return pl.BlockSpec(memory_space=pltpu.VMEM)


def beam_of(place, half_width, sky_cube, from_a, from_b):
    return pl.pallas_call(
        beam_kernel,
        out_shape=jax.ShapeDtypeStruct((4, 48, 1024), BF16),
        in_specs=[smem(), smem(), vmem(), vmem(), vmem()],
        out_specs=vmem(),
        compiler_params=params(),
        cost_estimate=pl.CostEstimate(flops=2 * 10**9, bytes_accessed=2**20, transcendentals=10**5),
        name="beam",
    )(place, half_width, sky_cube, from_a, from_b)


def three_shifts(beam):
    wide = beam.astype(F32)
    return jnp.concatenate([shift_cols(wide, e - 1).astype(BF16) for e in range(3)], axis=0)


def pick_taps(gram, first_group):
    n = gram.shape[1]
    shape = (512, n)
    diff = iota(shape, 1) % 48 - iota(shape, 0) % 32
    total = jnp.zeros((16, 128), F32)
    for b in range(3):
        part = jnp.where(diff == b, gram, 0.0).reshape(16, 32, n).sum(axis=1)
        group = iota((n, 128), 0) // 48 + first_group
        tap = 9 * (group // 3) + 3 * b + group % 3
        chosen = (iota((n, 128), 1) % 32 == tap).astype(F32)
        total = total + jnp.dot(part, chosen, preferred_element_type=F32, precision=lax.Precision.HIGHEST)
    return total


def contract(a, b):
    return lax.dot_general(a, b, (((1,), (1,)), ((), ())), preferred_element_type=F32)


def inner_kernel(beam_ref, cot_ref, out_ref, shift_ref, gram_ref):
    f = pl.program_id(0)

    @pl.when(f == 0)
    def _():
        gram_ref[...] = jnp.zeros_like(gram_ref)
        shift_ref[pl.ds(0, 144)] = jnp.zeros((144, 1024), BF16)
        shift_ref[pl.ds(720, 144)] = jnp.zeros((144, 1024), BF16)
        for p in range(4):
            shift_ref[pl.ds(144 * (p + 1), 144)] = three_shifts(beam_ref[p])

    cot = cot_ref[...].reshape(512, 1024)
    start = pl.multiple_of(f * 144, 16)
    gram_ref[...] += contract(cot, shift_ref[pl.ds(start, 432)])

    @pl.when(f == pl.num_programs(0) - 1)
    def _():
        out_ref[...] = pick_taps(gram_ref[...], 0)


def inner_terms(beam, out_cotangent):
    return pl.pallas_call(
        inner_kernel,
        grid=(4,),
        out_shape=jax.ShapeDtypeStruct((16, 128), F32),
        in_specs=[
            pl.BlockSpec((4, 48, 1024), lambda f: (0, 0, 0)),
            pl.BlockSpec((16, 1, 32, 1024), lambda f: (0, f, 0, 0)),
        ],
        out_specs=pl.BlockSpec((16, 128), lambda f: (0, 0)),
        scratch_shapes=[pltpu.VMEM((864, 1024), BF16), pltpu.VMEM((512, 432), F32)],
        compiler_params=params(),
        cost_estimate=pl.CostEstimate(flops=3 * 10**9, bytes_accessed=6 * 2**20, transcendentals=0),
        name="inner_terms",
    )(beam, out_cotangent)


def outer_kernel(where_ref, inner_ref, core_ref, far_ref, first_ref, last_ref, out_ref):
    even = where_ref[1] % 2 == 0
    core, far = core_ref[...], far_ref[...]
    before = jnp.where(even, far, core)
    after = jnp.where(even, core, far)
    low = contract(first_ref[...].reshape(512, 1024), three_shifts(before))
    high = contract(last_ref[...].reshape(512, 1024), three_shifts(after))
    total = inner_ref[...] + pick_taps(low, 0) + pick_taps(high, 6)
    placed = jnp.where(iota((16, 128), 1) // 32 == iota((16, 128), 0) % 4, total, 0.0)
    packed = placed.reshape(4, 4, 128).sum(axis=1)
    out_ref[...] = jnp.broadcast_to(packed[None], out_ref.shape)


def outer_terms(place, inner, from_core, from_far, out_cotangent, copies):
    plane = (16, 1, 32, 1024)
    whole = lambda i: (0, 0)
    return pl.pallas_call(
        outer_kernel,
        grid=(1,),
        out_shape=jax.ShapeDtypeStruct((copies, 4, 128), F32),
        in_specs=[
            smem(),
            pl.BlockSpec((16, 128), whole),
            pl.BlockSpec((48, 1024), whole),
            pl.BlockSpec((48, 1024), whole),
            pl.BlockSpec(plane, lambda i: (0, 0, 0, 0)),
            pl.BlockSpec(plane, lambda i: (0, 3, 0, 0)),
        ],
        out_specs=pl.BlockSpec((copies, 4, 128), lambda i: (0, 0, 0)),
        compiler_params=params(),
        cost_estimate=pl.CostEstimate(flops=5 * 10**8, bytes_accessed=3 * 2**20, transcendentals=0),
        name="outer_terms",
    )(place, inner, from_core, from_far, out_cotangent, out_cotangent)


def spread_kernel(where_ref, width_ref, grad_ref, core_ref, far_ref, own_ref, up_ref, down_ref):
    even = where_ref[1] % 2 == 0
    core, far = core_ref[...], far_ref[...]
    row = iota((40, 1024), 0)
    first = jnp.where(where_ref[0] == 0, 1, 0)
    last = jnp.where(where_ref[0] == 31, 33, 34)
    keep = (row >= first) & (row < last)
    shared = (row < 2) | (row >= 32)
    for f in range(4):
        width = width_ref[f]
        grad = grad_ref[f + 1]
        if f == 0:
            grad = grad + jnp.where(even, far, core)
        if f == 3:
            grad = grad + jnp.where(even, core, far)
        grad = jnp.where(keep, grad, 0.0)
        hi = grad.astype(BF16).astype(F32)
        lo = jnp.where(shared, grad - hi, 0.0)
        both = jnp.concatenate([hi, lo], axis=0).astype(BF16)
        smooth = blur_columns(both, width)
        out = blur_rows(smooth[:40] + smooth[40:], 64, -15, width)
        up_ref[f] = out[:16]
        own_ref[f] = out[16:48]
        down_ref[f] = out[48:]


def spread(place, half_width, grad, from_core, from_far):
    return pl.pallas_call(
        spread_kernel,
        out_shape=(
            jax.ShapeDtypeStruct((4, 32, 1024), F32),
            jax.ShapeDtypeStruct((4, 16, 1024), F32),
            jax.ShapeDtypeStruct((4, 16, 1024), F32),
        ),
        in_specs=[smem(), smem(), vmem(), vmem(), vmem()],
        out_specs=(vmem(), vmem(), vmem()),
        compiler_params=params(),
        cost_estimate=pl.CostEstimate(flops=3 * 10**9, bytes_accessed=3 * 2**20, transcendentals=10**5),
        name="spread",
    )(place, half_width, grad, from_core, from_far)


def final_kernel(scale, where_ref, own_ref, a_ref, b_ref, terms_ref, sky_ref, grad_ref):
    even = where_ref[0] % 2 == 0
    for f in range(4):
        ra, rb = a_ref[f], b_ref[f]
        sky_ref[f, :HALF] = own_ref[f, :HALF] + jnp.where(even, rb, ra)
        sky_ref[f, HALF:] = own_ref[f, HALF:] + jnp.where(even, ra, rb)
    packed = jnp.sum(terms_ref[...], axis=0) * scale
    rows = jnp.broadcast_to(packed[:, None, :], (4, 4, 128)).reshape(16, 128)
    placed = jnp.where(iota((16, 128), 1) // 32 == iota((16, 128), 0) % 4, rows, 0.0)
    fold = (iota((128, 128), 0) % 32 == iota((128, 128), 1)).astype(F32)
    out = jnp.dot(placed, fold, preferred_element_type=F32, precision=lax.Precision.HIGHEST)
    grad_ref[...] = out[:, :27]


def finish(scale, place, own, from_a, from_b, terms):
    def body(*refs):
        final_kernel(scale, *refs)

    return pl.pallas_call(
        body,
        out_shape=(jax.ShapeDtypeStruct((4, 32, 1024), F32), jax.ShapeDtypeStruct((16, 27), F32)),
        in_specs=[smem()] + [vmem()] * 4,
        out_specs=(vmem(), vmem()),
        compiler_params=params(),
        cost_estimate=pl.CostEstimate(flops=10**6, bytes_accessed=2 * 2**20, transcendentals=0),
        name="finish",
    )(place, own, from_a, from_b, terms)


def pair_swap(x, axis, odd_pairs):
    size = lax.axis_size(axis)
    first = 1 if odd_pairs else 0
    pairs = [(i, i + 1) for i in range(first, size - 1, 2)]
    return lax.ppermute(x, axis, pairs + [(j, i) for i, j in pairs])


def per_device(sky_cube, half_width, conv_weight, out_cotangent):
    freq_count, row_count, length = sky_cube.shape
    s, f = lax.axis_index("sky"), lax.axis_index("freq")
    place = jnp.stack([s, f]).astype(jnp.int32)
    s_even, f_even = s % 2 == 0, f % 2 == 0

    low_rows, high_rows = sky_cube[:, :HALF], sky_cube[:, HALF:]
    sky_b = pair_swap(jnp.where(s_even, low_rows, high_rows), "sky", True)
    sky_a = pair_swap(jnp.where(s_even, high_rows, low_rows), "sky", False)
    grad = back_project(conv_weight, out_cotangent)
    beam = beam_of(place, half_width, sky_cube, sky_a, sky_b)

    to_core = jnp.where(f_even, beam[3], beam[0])
    to_far = jnp.where(f_even, beam[0], beam[3])
    grad_core = jnp.where(f_even, grad[5], grad[0])
    grad_far = jnp.where(f_even, grad[0], grad[5])
    beam_far, add_far = pair_swap(to_far, "freq", True), pair_swap(grad_far, "freq", True)
    beam_core, add_core = pair_swap(to_core, "freq", False), pair_swap(grad_core, "freq", False)
    inner = inner_terms(beam, out_cotangent)

    own, up, down = spread(place, half_width, grad, add_core, add_far)
    row_b = pair_swap(jnp.where(s_even, up, down), "sky", True)
    row_a = pair_swap(jnp.where(s_even, down, up), "sky", False)
    copies = lax.axis_size("freq") * lax.axis_size("sky")
    terms = outer_terms(place, inner, beam_core, beam_far, out_cotangent, copies)
    gathered = lax.all_to_all(terms, ("freq", "sky"), 0, 0)
    cell_count = freq_count * lax.axis_size("freq") * row_count * lax.axis_size("sky") * length
    return finish(1.0 / math.sqrt(cell_count), place, own, row_a, row_b, gathered)


def solution(mesh):
    return jax.shard_map(
        per_device,
        mesh=mesh,
        in_specs=(P("freq", "sky", None), P("freq"), P(), P(None, "freq", "sky", None)),
        out_specs=(P("freq", "sky", None), P()),
        check_vma=False,
    )
```

```python
import math

import jax
import jax.numpy as jnp
from jax import lax
from jax.experimental import pallas as pl
from jax.experimental.pallas import tpu as pltpu
from jax.sharding import PartitionSpec as P

MAXH = 12
HALF = 16
F32 = jnp.float32
BF16 = jnp.bfloat16
MIB = 1024 * 1024


def params(mib=24):
    return pltpu.CompilerParams(vmem_limit_bytes=mib * MIB)


def iota(shape, dim):
    return lax.broadcasted_iota(jnp.int32, shape, dim)


def dot(a, b):
    return jnp.dot(a, b, preferred_element_type=F32)


def split(x):
    hi = x.astype(BF16)
    return hi, (x - hi.astype(F32)).astype(BF16)


def taps_at(offsets, width):
    def profile(d):
        w = jnp.full(d.shape, width, jnp.int32)
        wf = w.astype(F32)
        df = d.astype(F32)
        return jnp.where(jnp.abs(d) <= w, jnp.exp(-2.0 * (df * df) / (wf * wf)), 0.0)

    line = profile(iota((8, 128), 1) - 64)
    norm = jnp.sqrt(jnp.sum(line * line, axis=1, keepdims=True))[:1]
    return profile(offsets) / norm


def column_matrices(width):
    band = taps_at(iota((160, 128), 0) - 16 - iota((160, 128), 1), width)
    left = jnp.concatenate([jnp.zeros((112, 128), F32), band, jnp.zeros((240, 128), F32)], axis=0)
    right = jnp.concatenate([jnp.zeros((240, 128), F32), band, jnp.zeros((112, 128), F32)], axis=0)
    return split(jnp.concatenate([left, right], axis=1))


def blur_columns(rows, hi, lo):
    n = rows.shape[0]
    edge = jnp.zeros((n, 128), BF16)
    padded = jnp.concatenate([edge, rows, edge], axis=1)
    stacked = jnp.concatenate([padded[:, 256 * j : 256 * j + 512] for j in range(4)], axis=0)
    out = dot(stacked, hi) + dot(stacked, lo)
    return jnp.concatenate([out[n * j : n * j + n] for j in range(4)], axis=1)


def row_matrix(count, n, base, width):
    hi, lo = split(taps_at(iota((count, n), 1) - iota((count, n), 0) - base, width))
    hi, lo = hi.astype(F32), lo.astype(F32)
    return jnp.concatenate([hi, hi, lo], axis=1).astype(BF16)


def three_parts(source):
    hi = source.astype(BF16).astype(F32)
    return jnp.concatenate([hi, source - hi, hi], axis=0).astype(BF16)


def shift_cols(x, offset):
    if offset == 0:
        return x
    length = x.shape[-1]
    col = iota(x.shape, x.ndim - 1)
    if offset > 0:
        return jnp.where(col < length - 1, pltpu.roll(x, length - 1, x.ndim - 1), 0.0)
    return jnp.where(col > 0, pltpu.roll(x, 1, x.ndim - 1), 0.0)


def vmem():
    return pl.BlockSpec(memory_space=pltpu.VMEM)


def hbm():
    return pl.BlockSpec(memory_space=pltpu.HBM)


def plane_copies(cot_ref, planes, held, sem):
    return [pltpu.make_async_copy(cot_ref.at[:, f], held.at[i], sem.at[i]) for i, f in enumerate(planes)]


def back_kernel(
    width_hbm, weight_hbm, cot_ref, out_ref, mats_ref, held, acc_ref, weight_ref, width_ref, sem
):
    small = [
        pltpu.make_async_copy(weight_hbm, weight_ref, sem.at[4]),
        pltpu.make_async_copy(width_hbm, width_ref, sem.at[5]),
    ]
    for copy in small:
        copy.start()
    copies = plane_copies(cot_ref, range(4), held, sem)
    for copy in copies:
        copy.start()
    small[0].wait()
    small[1].wait()
    expand = (iota((16, 512), 1) // 32 == iota((16, 512), 0)).astype(BF16)
    w = lax.dot_general(weight_ref[...], expand, (((0,), (0,)), ((), ())), preferred_element_type=F32)
    diff = iota((40, 512), 0) - iota((40, 512), 1) % 32
    blocks = []
    for a in range(3):
        for e in range(3):
            block = jnp.zeros((40, 512), F32)
            for b in range(3):
                row = w[9 * a + 3 * b + e : 9 * a + 3 * b + e + 1, :]
                block = jnp.where(diff == b, row, block)
            blocks.append(block)
    matrix = jnp.concatenate(blocks, axis=0).astype(BF16)
    for f in range(4):
        width = width_ref[f]
        mats_ref[f, :512], mats_ref[f, 512:1024] = column_matrices(width)
        mats_ref[f, 1024:1072, :192] = row_matrix(48, 64, 15, width)
        mats_ref[f, 1072:, :120] = row_matrix(64, 40, -15, width)
    for f in range(4):
        copies[f].wait()
        terms = dot(matrix, held[f].reshape(512, 1024))
        for a in range(3):
            part = terms[120 * a : 120 * a + 120]
            if f == 0 or a == 2:
                acc_ref[f + a] = part
            else:
                acc_ref[f + a] += part
    for p in range(6):
        full = acc_ref[p]
        out_ref[p] = shift_cols(full[0:40], 1) + full[40:80] + shift_cols(full[80:120], -1)


def back_project(half_width, conv_weight, out_cotangent):
    return pl.pallas_call(
        back_kernel,
        out_shape=(
            jax.ShapeDtypeStruct((6, 40, 1024), F32),
            jax.ShapeDtypeStruct((4, 1136, 256), BF16),
            jax.ShapeDtypeStruct((4, 16, 32, 1024), BF16),
        ),
        in_specs=[hbm(), hbm(), hbm()],
        out_specs=(vmem(),) * 3,
        scratch_shapes=[
            pltpu.VMEM((6, 120, 1024), F32),
            pltpu.VMEM((16, 27), BF16),
            pltpu.SMEM((4,), jnp.int32),
            pltpu.SemaphoreType.DMA((6,)),
        ],
        compiler_params=params(),
        cost_estimate=pl.CostEstimate(flops=3 * 10**9, bytes_accessed=7 * 2**20, transcendentals=10**5),
        name="back_project",
    )(half_width, conv_weight, out_cotangent)


def beam_kernel(mats_ref, sky_ref, a_ref, b_ref, grad_ref, beam_ref, core_ref, far_ref):
    even = lax.axis_index("sky") % 2 == 0
    f_even = lax.axis_index("freq") % 2 == 0
    row = iota((48, 1024), 0)
    first = jnp.where(lax.axis_index("sky") == 0, 1, 0)
    last = jnp.where(lax.axis_index("sky") == lax.axis_size("sky") - 1, 33, 34)
    keep = (row >= first) & (row < last)
    smooth = []
    for f in range(4):
        ra, rb = a_ref[f], b_ref[f]
        above = jnp.where(even, rb, ra)
        below = jnp.where(even, ra, rb)
        rows = jnp.concatenate([above, sky_ref[f], below], axis=0)
        smooth.append(three_parts(blur_columns(rows, mats_ref[f, :512], mats_ref[f, 512:1024])))
    beams = [jnp.where(keep, dot(mats_ref[f, 1024:1072, :192], smooth[f]), 0.0) for f in range(4)]
    for f in range(4):
        beam_ref[f] = beams[f].astype(BF16)
    edges = []
    for f, p in ((0, 0), (3, 5)):
        g = grad_ref[p]
        high = g.astype(BF16).astype(F32)
        edges.append(jnp.concatenate([beams[f], high, g - high], axis=0))
    core_ref[...] = jnp.where(f_even, edges[1], edges[0]).astype(BF16)
    far_ref[...] = jnp.where(f_even, edges[0], edges[1]).astype(BF16)


def beam_of(mats, sky_cube, from_a, from_b, grad):
    edge = jax.ShapeDtypeStruct((128, 1024), BF16)
    return pl.pallas_call(
        beam_kernel,
        out_shape=(jax.ShapeDtypeStruct((4, 48, 1024), BF16), edge, edge),
        in_specs=[vmem()] * 5,
        out_specs=(vmem(), vmem(), vmem()),
        compiler_params=params(),
        cost_estimate=pl.CostEstimate(flops=10**9, bytes_accessed=4 * 2**20, transcendentals=0),
        name="beam",
    )(mats, sky_cube, from_a, from_b, grad)


def three_shifts(beam):
    wide = beam[:40].astype(F32)
    parts = [shift_cols(wide, e - 1) for e in range(3)] + [jnp.zeros((8, beam.shape[1]), F32)]
    return jnp.concatenate(parts, axis=0).astype(BF16)


def contract(a, b):
    return lax.dot_general(a, b, (((1,), (1,)), ((), ())), preferred_element_type=F32)


def inner_kernel(beam_ref, cot_ref, out_ref, shift_ref):
    for p in range(4):
        shift_ref[pl.ds(128 * p, 128)] = three_shifts(beam_ref[p])
    for f in (1, 0, 2, 3):
        low, high = max(f - 1, 0), min(f + 2, 4)
        terms = contract(cot_ref[f].reshape(512, 1024), shift_ref[pl.ds(128 * low, 128 * (high - low))])
        cols = pl.ds(128 * (low - f + 1), 128 * (high - low))
        if f == 1:
            out_ref[:, cols] = terms
        else:
            out_ref[:, cols] += terms


def inner_terms(beam, out_cotangent):
    return pl.pallas_call(
        inner_kernel,
        out_shape=jax.ShapeDtypeStruct((512, 384), F32),
        in_specs=[vmem(), vmem()],
        out_specs=vmem(),
        scratch_shapes=[pltpu.VMEM((512, 1024), BF16)],
        compiler_params=params(),
        cost_estimate=pl.CostEstimate(flops=2 * 10**9, bytes_accessed=6 * 2**20, transcendentals=0),
        name="inner_terms",
    )(beam, out_cotangent)


def outer_kernel(gram_ref, core_ref, far_ref, cot_ref, out_ref):
    even = lax.axis_index("freq") % 2 == 0
    core, far = core_ref[:48], far_ref[:48]
    before = three_shifts(jnp.where(even, far, core))
    after = three_shifts(jnp.where(even, core, far))
    low = contract(cot_ref[0].reshape(512, 1024), before) + gram_ref[:, :128]
    high = contract(cot_ref[3].reshape(512, 1024), after) + gram_ref[:, 256:]
    gram = jnp.concatenate([low, gram_ref[:, 128:256], high], axis=1).reshape(16, 32, 384)
    col = iota((32, 384), 1) % 128
    e = col // 40
    diff = col - 40 * e - iota((32, 384), 0)
    parts = [jnp.where((diff == b)[None], gram, 0.0).sum(axis=1) for b in range(3)]
    sums = jnp.concatenate(parts, axis=1)
    top, rest = split(sums)
    rest = sums - top.astype(F32)
    mid = rest.astype(BF16)
    low_part = (rest - mid.astype(F32)).astype(BF16)
    n = iota((1152, 128), 0)
    b, a, e = n // 384, n % 384 // 128, n % 128 // 40
    chosen = (iota((1152, 128), 1) % 32 == jnp.where(e < 3, 9 * a + 3 * b + e, 99)).astype(F32).astype(BF16)
    total = dot(top, chosen) + (dot(mid, chosen) + dot(low_part, chosen))
    placed = jnp.where(iota((16, 128), 1) // 32 == iota((16, 128), 0) % 4, total, 0.0)
    packed = placed.reshape(4, 4, 128).sum(axis=1)
    out_ref[...] = jnp.broadcast_to(packed[None], out_ref.shape)


def outer_terms(gram, from_core, from_far, out_cotangent, copies):
    return pl.pallas_call(
        outer_kernel,
        out_shape=jax.ShapeDtypeStruct((copies, 4, 128), F32),
        in_specs=[vmem()] * 4,
        out_specs=vmem(),
        compiler_params=params(),
        cost_estimate=pl.CostEstimate(flops=5 * 10**8, bytes_accessed=3 * 2**20, transcendentals=0),
        name="outer_terms",
    )(gram, from_core, from_far, out_cotangent)


def spread_kernel(mats_ref, grad_ref, core_ref, far_ref, own_ref, to_a_ref, to_b_ref):
    s_even = lax.axis_index("sky") % 2 == 0
    even = lax.axis_index("freq") % 2 == 0
    core = core_ref[48:88].astype(F32) + core_ref[88:].astype(F32)
    far = far_ref[48:88].astype(F32) + far_ref[88:].astype(F32)
    row = iota((40, 1024), 0)
    first = jnp.where(lax.axis_index("sky") == 0, 1, 0)
    last = jnp.where(lax.axis_index("sky") == lax.axis_size("sky") - 1, 33, 34)
    keep = (row >= first) & (row < last)
    shared = (row < 2) | (row >= 32)
    smooth = []
    for f in range(4):
        grad = grad_ref[f + 1]
        if f == 0:
            grad = grad + jnp.where(even, far, core)
        if f == 3:
            grad = grad + jnp.where(even, core, far)
        grad = jnp.where(keep, grad, 0.0)
        hi = grad.astype(BF16).astype(F32)
        lo = jnp.where(shared, grad - hi, 0.0)
        both = blur_columns(jnp.concatenate([hi, lo], axis=0).astype(BF16), mats_ref[f, :512], mats_ref[f, 512:1024])
        smooth.append(three_parts(both[:40] + both[40:]))
    for f in range(4):
        out = dot(mats_ref[f, 1072:, :120], smooth[f])
        own_ref[f] = out[16:48]
        to_a_ref[f] = jnp.where(s_even, out[48:], out[:16])
        to_b_ref[f] = jnp.where(s_even, out[:16], out[48:])


def spread(mats, grad, from_core, from_far):
    edge = jax.ShapeDtypeStruct((4, HALF, 1024), F32)
    return pl.pallas_call(
        spread_kernel,
        out_shape=(jax.ShapeDtypeStruct((4, 32, 1024), F32), edge, edge),
        in_specs=[vmem()] * 4,
        out_specs=(vmem(), vmem(), vmem()),
        compiler_params=params(),
        cost_estimate=pl.CostEstimate(flops=10**9, bytes_accessed=3 * 2**20, transcendentals=0),
        name="spread",
    )(mats, grad, from_core, from_far)


def final_kernel(scale, own_ref, a_ref, b_ref, terms_ref, sky_ref, grad_ref):
    even = lax.axis_index("sky") % 2 == 0
    for f in range(4):
        ra, rb = a_ref[f], b_ref[f]
        sky_ref[f, :HALF] = own_ref[f, :HALF] + jnp.where(even, rb, ra)
        sky_ref[f, HALF:] = own_ref[f, HALF:] + jnp.where(even, ra, rb)
    packed = jnp.sum(terms_ref[...], axis=0) * scale
    rows = jnp.broadcast_to(packed[:, None, :], (4, 4, 128)).reshape(16, 128)
    placed = jnp.where(iota((16, 128), 1) // 32 == iota((16, 128), 0) % 4, rows, 0.0)
    fold = (iota((128, 128), 0) % 32 == iota((128, 128), 1)).astype(F32)
    out = jnp.dot(placed, fold, preferred_element_type=F32, precision=lax.Precision.HIGHEST)
    grad_ref[...] = out[:, :27]


def finish(scale, own, from_a, from_b, terms):
    def body(*refs):
        final_kernel(scale, *refs)

    return pl.pallas_call(
        body,
        out_shape=(jax.ShapeDtypeStruct((4, 32, 1024), F32), jax.ShapeDtypeStruct((16, 27), F32)),
        in_specs=[vmem()] * 4,
        out_specs=(vmem(), vmem()),
        compiler_params=params(),
        cost_estimate=pl.CostEstimate(flops=10**6, bytes_accessed=2 * 2**20, transcendentals=0),
        name="finish",
    )(own, from_a, from_b, terms)


def pair_swap(x, axis, odd_pairs):
    size = lax.axis_size(axis)
    first = 1 if odd_pairs else 0
    pairs = [(i, i + 1) for i in range(first, size - 1, 2)]
    return lax.ppermute(x, axis, pairs + [(j, i) for i, j in pairs])


def per_device(sky_cube, half_width, conv_weight, out_cotangent):
    freq_count, row_count, length = sky_cube.shape
    s_even = lax.axis_index("sky") % 2 == 0
    out_cotangent, conv_weight, half_width = (
        pltpu.with_memory_space_constraint(x, pltpu.HBM) for x in (out_cotangent, conv_weight, half_width)
    )

    low_rows, high_rows = sky_cube[:, :HALF], sky_cube[:, HALF:]
    sky_a = pair_swap(jnp.where(s_even, high_rows, low_rows), "sky", False)
    sky_b = pair_swap(jnp.where(s_even, low_rows, high_rows), "sky", True)
    grad, mats, held = back_project(half_width, conv_weight, out_cotangent)
    beam, to_core, to_far = beam_of(mats, sky_cube, sky_a, sky_b, grad)
    from_core, from_far = pair_swap(to_core, "freq", False), pair_swap(to_far, "freq", True)
    gram = inner_terms(beam, held)
    own, to_a, to_b = spread(mats, grad, from_core, from_far)
    row_a, row_b = pair_swap(to_a, "sky", False), pair_swap(to_b, "sky", True)
    copies = lax.axis_size("freq") * lax.axis_size("sky")
    terms = outer_terms(gram, from_core, from_far, held, copies)
    gathered = lax.all_to_all(terms, ("freq", "sky"), 0, 0)
    cell_count = freq_count * lax.axis_size("freq") * row_count * lax.axis_size("sky") * length
    return finish(1.0 / math.sqrt(cell_count), own, row_a, row_b, gathered)


def solution(mesh):
    return jax.shard_map(
        per_device,
        mesh=mesh,
        in_specs=(P("freq", "sky", None), P("freq"), P(), P(None, "freq", "sky", None)),
        out_specs=(P("freq", "sky", None), P()),
        check_vma=False,
    )
```

```python
import math

import jax
import jax.numpy as jnp
from jax import lax
from jax.experimental import pallas as pl
from jax.experimental.pallas import tpu as pltpu
from jax.sharding import PartitionSpec as P

MAXH = 12
HALF = 16
F32 = jnp.float32
BF16 = jnp.bfloat16
MIB = 1024 * 1024


def params(mib=24):
    return pltpu.CompilerParams(vmem_limit_bytes=mib * MIB)


def iota(shape, dim):
    return lax.broadcasted_iota(jnp.int32, shape, dim)


def dot(a, b):
    return jnp.dot(a, b, preferred_element_type=F32)


def split(x):
    hi = x.astype(BF16)
    return hi, (x - hi.astype(F32)).astype(BF16)


def taps_at(offsets, width):
    def profile(d):
        w = jnp.full(d.shape, width, jnp.int32)
        wf = w.astype(F32)
        df = d.astype(F32)
        return jnp.where(jnp.abs(d) <= w, jnp.exp(-2.0 * (df * df) / (wf * wf)), 0.0)

    line = profile(iota((8, 128), 1) - 64)
    norm = jnp.sqrt(jnp.sum(line * line, axis=1, keepdims=True))[:1]
    return profile(offsets) / norm


def column_matrices(width):
    band = taps_at(iota((160, 128), 0) - 16 - iota((160, 128), 1), width)
    left = jnp.concatenate([jnp.zeros((112, 128), F32), band, jnp.zeros((240, 128), F32)], axis=0)
    right = jnp.concatenate([jnp.zeros((240, 128), F32), band, jnp.zeros((112, 128), F32)], axis=0)
    return split(jnp.concatenate([left, right], axis=1))


def blur_columns(rows, hi, lo):
    n = rows.shape[0]
    edge = jnp.zeros((n, 128), BF16)
    padded = jnp.concatenate([edge, rows, edge], axis=1)
    stacked = jnp.concatenate([padded[:, 256 * j : 256 * j + 512] for j in range(4)], axis=0)
    out = dot(stacked, hi) + dot(stacked, lo)
    return jnp.concatenate([out[n * j : n * j + n] for j in range(4)], axis=1)


def row_matrix(count, n, base, width):
    hi, lo = split(taps_at(iota((count, n), 1) - iota((count, n), 0) - base, width))
    hi, lo = hi.astype(F32), lo.astype(F32)
    return jnp.concatenate([hi, hi, lo], axis=1).astype(BF16)


def three_parts(source):
    hi = source.astype(BF16).astype(F32)
    return jnp.concatenate([hi, source - hi, hi], axis=0).astype(BF16)


def shift_cols(x, offset):
    if offset == 0:
        return x
    length = x.shape[-1]
    col = iota(x.shape, x.ndim - 1)
    if offset > 0:
        return jnp.where(col < length - 1, pltpu.roll(x, length - 1, x.ndim - 1), 0.0)
    return jnp.where(col > 0, pltpu.roll(x, 1, x.ndim - 1), 0.0)


def vmem():
    return pl.BlockSpec(memory_space=pltpu.VMEM)


def hbm():
    return pl.BlockSpec(memory_space=pltpu.HBM)


def plane_copies(cot_ref, planes, held, sem):
    return [pltpu.make_async_copy(cot_ref.at[:, f], held.at[i], sem.at[i]) for i, f in enumerate(planes)]


def back_kernel(
    width_hbm, weight_hbm, cot_ref, out_ref, mats_ref, held, acc_ref, weight_ref, width_ref, sem
):
    small = [
        pltpu.make_async_copy(weight_hbm, weight_ref, sem.at[4]),
        pltpu.make_async_copy(width_hbm, width_ref, sem.at[5]),
    ]
    for copy in small:
        copy.start()
    copies = plane_copies(cot_ref, range(4), held, sem)
    for copy in copies:
        copy.start()
    small[0].wait()
    small[1].wait()
    expand = (iota((16, 512), 1) // 32 == iota((16, 512), 0)).astype(BF16)
    w = lax.dot_general(weight_ref[...], expand, (((0,), (0,)), ((), ())), preferred_element_type=F32)
    diff = iota((40, 512), 0) - iota((40, 512), 1) % 32
    blocks = []
    for a in range(3):
        for e in range(3):
            block = jnp.zeros((40, 512), F32)
            for b in range(3):
                row = w[9 * a + 3 * b + e : 9 * a + 3 * b + e + 1, :]
                block = jnp.where(diff == b, row, block)
            blocks.append(block)
    matrix = jnp.concatenate(blocks, axis=0).astype(BF16)
    for f in range(4):
        width = width_ref[f]
        mats_ref[f, :512], mats_ref[f, 512:1024] = column_matrices(width)
        mats_ref[f, 1024:1072, :192] = row_matrix(48, 64, 15, width)
        mats_ref[f, 1072:, :120] = row_matrix(64, 40, -15, width)
    for f in range(4):
        copies[f].wait()
        terms = dot(matrix, held[f].reshape(512, 1024))
        for a in range(3):
            part = terms[120 * a : 120 * a + 120]
            if f == 0 or a == 2:
                acc_ref[f + a] = part
            else:
                acc_ref[f + a] += part
    for p in range(6):
        full = acc_ref[p]
        out_ref[p] = shift_cols(full[0:40], 1) + full[40:80] + shift_cols(full[80:120], -1)


def back_project(half_width, conv_weight, out_cotangent):
    return pl.pallas_call(
        back_kernel,
        out_shape=(
            jax.ShapeDtypeStruct((6, 40, 1024), F32),
            jax.ShapeDtypeStruct((4, 1136, 256), BF16),
            jax.ShapeDtypeStruct((4, 16, 32, 1024), BF16),
        ),
        in_specs=[hbm(), hbm(), hbm()],
        out_specs=(vmem(),) * 3,
        scratch_shapes=[
            pltpu.VMEM((6, 120, 1024), F32),
            pltpu.VMEM((16, 27), BF16),
            pltpu.SMEM((4,), jnp.int32),
            pltpu.SemaphoreType.DMA((6,)),
        ],
        compiler_params=params(),
        cost_estimate=pl.CostEstimate(flops=3 * 10**9, bytes_accessed=7 * 2**20, transcendentals=10**5),
        name="back_project",
    )(half_width, conv_weight, out_cotangent)


def beam_kernel(mats_ref, sky_ref, b_ref, a_ref, grad_ref, beam_ref, core_ref, far_ref):
    even = lax.axis_index("sky") % 2 == 0
    f_even = lax.axis_index("freq") % 2 == 0
    row = iota((48, 1024), 0)
    first = jnp.where(lax.axis_index("sky") == 0, 1, 0)
    last = jnp.where(lax.axis_index("sky") == lax.axis_size("sky") - 1, 33, 34)
    keep = (row >= first) & (row < last)
    smooth = []
    for f in range(4):
        ra, rb = a_ref[f], b_ref[f]
        above = jnp.where(even, rb, ra)
        below = jnp.where(even, ra, rb)
        rows = jnp.concatenate([above, sky_ref[f], below], axis=0)
        smooth.append(three_parts(blur_columns(rows, mats_ref[f, :512], mats_ref[f, 512:1024])))
    beams = [jnp.where(keep, dot(mats_ref[f, 1024:1072, :192], smooth[f]), 0.0) for f in range(4)]
    for f in range(4):
        beam_ref[f] = beams[f].astype(BF16)
    edges = []
    for f, p in ((0, 0), (3, 5)):
        g = grad_ref[p]
        edges.append(jnp.concatenate([beams[f][:40], g], axis=0))
    core_ref[...] = jnp.where(f_even, edges[1], edges[0]).astype(BF16)
    far_ref[...] = jnp.where(f_even, edges[0], edges[1]).astype(BF16)


def beam_of(mats, sky_cube, from_b, from_a, grad):
    edge = jax.ShapeDtypeStruct((80, 1024), BF16)
    return pl.pallas_call(
        beam_kernel,
        out_shape=(jax.ShapeDtypeStruct((4, 48, 1024), BF16), edge, edge),
        in_specs=[vmem()] * 5,
        out_specs=(vmem(), vmem(), vmem()),
        compiler_params=params(),
        cost_estimate=pl.CostEstimate(flops=10**9, bytes_accessed=4 * 2**20, transcendentals=0),
        name="beam",
    )(mats, sky_cube, from_b, from_a, grad)


def three_shifts(beam):
    wide = beam[:40].astype(F32)
    parts = [shift_cols(wide, e - 1) for e in range(3)] + [jnp.zeros((8, beam.shape[1]), F32)]
    return jnp.concatenate(parts, axis=0).astype(BF16)


def contract(a, b):
    return lax.dot_general(a, b, (((1,), (1,)), ((), ())), preferred_element_type=F32)


def pick_taps(gram, step):
    n = gram.shape[1]
    col = iota((4, 8, n), 2) % 128
    diff = col - 40 * (col // 40) - (iota((4, 8, n), 0) * 8 + iota((4, 8, n), 1))
    tiles = gram.reshape(16, 4, 8, n)
    parts = [jnp.where((diff == b)[None], tiles, 0.0).sum(axis=1) for b in range(3)]
    sums = jnp.concatenate(parts, axis=2).reshape(128, 3 * n)
    top = sums.astype(BF16)
    rest = sums - top.astype(F32)
    mid = rest.astype(BF16)
    low = (rest - mid.astype(F32)).astype(BF16)
    i = iota((3 * n, 128), 0)
    b, a, e = i // n, step * (i % n // 128), i % 128 // 40
    chosen = (iota((3 * n, 128), 1) % 32 == jnp.where(e < 3, 9 * a + 3 * b + e, 99)).astype(F32).astype(BF16)
    total = dot(top, chosen) + (dot(mid, chosen) + dot(low, chosen))
    return total.reshape(16, 8, 128).sum(axis=1)


def inner_kernel(beam_ref, cot_ref, out_ref, shift_ref, gram_ref):
    for p in range(4):
        shift_ref[pl.ds(128 * p, 128)] = three_shifts(beam_ref[p])
    for f in (1, 0, 2, 3):
        low, high = max(f - 1, 0), min(f + 2, 4)
        terms = contract(cot_ref[f].reshape(512, 1024), shift_ref[pl.ds(128 * low, 128 * (high - low))])
        cols = pl.ds(128 * (low - f + 1), 128 * (high - low))
        if f == 1:
            gram_ref[:, cols] = terms
        else:
            gram_ref[:, cols] += terms
    out_ref[...] = pick_taps(gram_ref[...], 1)


def inner_terms(beam, out_cotangent):
    return pl.pallas_call(
        inner_kernel,
        out_shape=jax.ShapeDtypeStruct((16, 128), F32),
        in_specs=[vmem(), vmem()],
        out_specs=vmem(),
        scratch_shapes=[pltpu.VMEM((512, 1024), BF16), pltpu.VMEM((512, 384), F32)],
        compiler_params=params(),
        cost_estimate=pl.CostEstimate(flops=2 * 10**9, bytes_accessed=6 * 2**20, transcendentals=0),
        name="inner_terms",
    )(beam, out_cotangent)


def outer_kernel(inner_ref, core_ref, far_ref, cot_ref, out_ref):
    even = lax.axis_index("freq") % 2 == 0
    core, far = core_ref[:40], far_ref[:40]
    before = three_shifts(jnp.where(even, far, core))
    after = three_shifts(jnp.where(even, core, far))
    low = contract(cot_ref[0].reshape(512, 1024), before)
    high = contract(cot_ref[3].reshape(512, 1024), after)
    total = inner_ref[...] + pick_taps(jnp.concatenate([low, high], axis=1), 2)
    placed = jnp.where(iota((16, 128), 1) // 32 == iota((16, 128), 0) % 4, total, 0.0)
    packed = placed.reshape(4, 4, 128).sum(axis=1)
    out_ref[...] = jnp.broadcast_to(packed[None], out_ref.shape)


def outer_terms(inner, from_core, from_far, out_cotangent, copies):
    return pl.pallas_call(
        outer_kernel,
        out_shape=jax.ShapeDtypeStruct((copies, 4, 128), F32),
        in_specs=[vmem()] * 4,
        out_specs=vmem(),
        compiler_params=params(),
        cost_estimate=pl.CostEstimate(flops=5 * 10**8, bytes_accessed=3 * 2**20, transcendentals=0),
        name="outer_terms",
    )(inner, from_core, from_far, out_cotangent)


def spread_kernel(mats_ref, grad_ref, core_ref, far_ref, own_ref, to_a_ref, to_b_ref):
    s_even = lax.axis_index("sky") % 2 == 0
    even = lax.axis_index("freq") % 2 == 0
    core = core_ref[40:].astype(F32)
    far = far_ref[40:].astype(F32)
    row = iota((40, 1024), 0)
    first = jnp.where(lax.axis_index("sky") == 0, 1, 0)
    last = jnp.where(lax.axis_index("sky") == lax.axis_size("sky") - 1, 33, 34)
    keep = (row >= first) & (row < last)
    shared = (row < 2) | (row >= 32)
    smooth = []
    for f in range(4):
        grad = grad_ref[f + 1]
        if f == 0:
            grad = grad + jnp.where(even, far, core)
        if f == 3:
            grad = grad + jnp.where(even, core, far)
        grad = jnp.where(keep, grad, 0.0)
        hi = grad.astype(BF16).astype(F32)
        lo = jnp.where(shared, grad - hi, 0.0)
        both = blur_columns(jnp.concatenate([hi, lo], axis=0).astype(BF16), mats_ref[f, :512], mats_ref[f, 512:1024])
        smooth.append(three_parts(both[:40] + both[40:]))
    for f in range(4):
        out = dot(mats_ref[f, 1072:, :120], smooth[f])
        own_ref[f] = out[16:48]
        to_a_ref[f] = jnp.where(s_even, out[48:], out[:16])
        to_b_ref[f] = jnp.where(s_even, out[:16], out[48:])


def spread(mats, grad, from_core, from_far):
    edge = jax.ShapeDtypeStruct((4, HALF, 1024), F32)
    return pl.pallas_call(
        spread_kernel,
        out_shape=(jax.ShapeDtypeStruct((4, 32, 1024), F32), edge, edge),
        in_specs=[vmem()] * 4,
        out_specs=(vmem(), vmem(), vmem()),
        compiler_params=params(),
        cost_estimate=pl.CostEstimate(flops=10**9, bytes_accessed=3 * 2**20, transcendentals=0),
        name="spread",
    )(mats, grad, from_core, from_far)


def final_kernel(scale, own_ref, a_ref, b_ref, terms_ref, sky_ref, grad_ref):
    even = lax.axis_index("sky") % 2 == 0
    for f in range(4):
        ra, rb = a_ref[f], b_ref[f]
        sky_ref[f, :HALF] = own_ref[f, :HALF] + jnp.where(even, rb, ra)
        sky_ref[f, HALF:] = own_ref[f, HALF:] + jnp.where(even, ra, rb)
    packed = jnp.sum(terms_ref[...], axis=0) * scale
    rows = jnp.broadcast_to(packed[:, None, :], (4, 4, 128)).reshape(16, 128)
    placed = jnp.where(iota((16, 128), 1) // 32 == iota((16, 128), 0) % 4, rows, 0.0)
    fold = (iota((128, 128), 0) % 32 == iota((128, 128), 1)).astype(F32)
    out = jnp.dot(placed, fold, preferred_element_type=F32, precision=lax.Precision.HIGHEST)
    grad_ref[...] = out[:, :27]


def finish(scale, own, from_a, from_b, terms):
    def body(*refs):
        final_kernel(scale, *refs)

    return pl.pallas_call(
        body,
        out_shape=(jax.ShapeDtypeStruct((4, 32, 1024), F32), jax.ShapeDtypeStruct((16, 27), F32)),
        in_specs=[vmem()] * 4,
        out_specs=(vmem(), vmem()),
        compiler_params=params(),
        cost_estimate=pl.CostEstimate(flops=10**6, bytes_accessed=2 * 2**20, transcendentals=0),
        name="finish",
    )(own, from_a, from_b, terms)


def pair_swap(x, axis, odd_pairs):
    size = lax.axis_size(axis)
    first = 1 if odd_pairs else 0
    pairs = [(i, i + 1) for i in range(first, size - 1, 2)]
    return lax.ppermute(x, axis, pairs + [(j, i) for i, j in pairs])


def per_device(sky_cube, half_width, conv_weight, out_cotangent):
    freq_count, row_count, length = sky_cube.shape
    s_even = lax.axis_index("sky") % 2 == 0
    out_cotangent, conv_weight, half_width = (
        pltpu.with_memory_space_constraint(x, pltpu.HBM) for x in (out_cotangent, conv_weight, half_width)
    )

    low_rows, high_rows = sky_cube[:, :HALF], sky_cube[:, HALF:]
    sky_a = pair_swap(jnp.where(s_even, high_rows, low_rows), "sky", False)
    sky_b = pair_swap(jnp.where(s_even, low_rows, high_rows), "sky", True)
    grad, mats, held = back_project(half_width, conv_weight, out_cotangent)
    beam, to_core, to_far = beam_of(mats, sky_cube, sky_b, sky_a, grad)
    from_core, from_far = pair_swap(to_core, "freq", False), pair_swap(to_far, "freq", True)
    inner = inner_terms(beam, held)
    own, to_a, to_b = spread(mats, grad, from_core, from_far)
    row_a, row_b = pair_swap(to_a, "sky", False), pair_swap(to_b, "sky", True)
    copies = lax.axis_size("freq") * lax.axis_size("sky")
    terms = outer_terms(inner, from_core, from_far, held, copies)
    gathered = lax.all_to_all(terms, ("freq", "sky"), 0, 0)
    cell_count = freq_count * lax.axis_size("freq") * row_count * lax.axis_size("sky") * length
    return finish(1.0 / math.sqrt(cell_count), own, row_a, row_b, gathered)


def solution(mesh):
    return jax.shard_map(
        per_device,
        mesh=mesh,
        in_specs=(P("freq", "sky", None), P("freq"), P(), P(None, "freq", "sky", None)),
        out_specs=(P("freq", "sky", None), P()),
        check_vma=False,
    )
```

```python
import math

import jax
import jax.numpy as jnp
from jax import lax
from jax.experimental import pallas as pl
from jax.experimental.pallas import tpu as pltpu
from jax.sharding import PartitionSpec as P

MAXH = 12
HALF = 16
F32 = jnp.float32
BF16 = jnp.bfloat16
MIB = 1024 * 1024


def params(mib=24):
    return pltpu.CompilerParams(vmem_limit_bytes=mib * MIB)


def iota(shape, dim):
    return lax.broadcasted_iota(jnp.int32, shape, dim)


def dot(a, b):
    return jnp.dot(a, b, preferred_element_type=F32)


def split(x):
    hi = x.astype(BF16)
    return hi, (x - hi.astype(F32)).astype(BF16)


def taps_at(offsets, width):
    def profile(d):
        w = jnp.full(d.shape, width, jnp.int32)
        wf = w.astype(F32)
        df = d.astype(F32)
        return jnp.where(jnp.abs(d) <= w, jnp.exp(-2.0 * (df * df) / (wf * wf)), 0.0)

    line = profile(iota((8, 128), 1) - 64)
    norm = jnp.sqrt(jnp.sum(line * line, axis=1, keepdims=True))[:1]
    return profile(offsets) / norm


def column_matrices(width):
    band = taps_at(iota((160, 128), 0) - 16 - iota((160, 128), 1), width)
    left = jnp.concatenate([jnp.zeros((112, 128), F32), band, jnp.zeros((240, 128), F32)], axis=0)
    right = jnp.concatenate([jnp.zeros((240, 128), F32), band, jnp.zeros((112, 128), F32)], axis=0)
    return split(jnp.concatenate([left, right], axis=1))


def blur_columns(rows, hi, lo):
    n = rows.shape[0]
    edge = jnp.zeros((n, 128), BF16)
    padded = jnp.concatenate([edge, rows, edge], axis=1)
    stacked = jnp.concatenate([padded[:, 256 * j : 256 * j + 512] for j in range(4)], axis=0)
    out = dot(stacked, hi) + dot(stacked, lo)
    return jnp.concatenate([out[n * j : n * j + n] for j in range(4)], axis=1)


def row_matrix(count, n, base, width):
    hi, lo = split(taps_at(iota((count, n), 1) - iota((count, n), 0) - base, width))
    hi, lo = hi.astype(F32), lo.astype(F32)
    return jnp.concatenate([hi, hi, lo], axis=1).astype(BF16)


def three_parts(source):
    hi = source.astype(BF16).astype(F32)
    return jnp.concatenate([hi, source - hi, hi], axis=0).astype(BF16)


def shift_cols(x, offset):
    if offset == 0:
        return x
    length = x.shape[-1]
    col = iota(x.shape, x.ndim - 1)
    if offset > 0:
        return jnp.where(col < length - 1, pltpu.roll(x, length - 1, x.ndim - 1), 0.0)
    return jnp.where(col > 0, pltpu.roll(x, 1, x.ndim - 1), 0.0)


def vmem():
    return pl.BlockSpec(memory_space=pltpu.VMEM)


def hbm():
    return pl.BlockSpec(memory_space=pltpu.HBM)


def plane_copies(cot_ref, planes, held, sem):
    return [pltpu.make_async_copy(cot_ref.at[:, f], held.at[i], sem.at[i]) for i, f in enumerate(planes)]


def back_kernel(
    width_hbm, weight_hbm, cot_ref, out_ref, mats_ref, held, acc_ref, weight_ref, width_ref, sem
):
    small = [
        pltpu.make_async_copy(weight_hbm, weight_ref, sem.at[4]),
        pltpu.make_async_copy(width_hbm, width_ref, sem.at[5]),
    ]
    for copy in small:
        copy.start()
    copies = plane_copies(cot_ref, range(4), held, sem)
    for copy in copies:
        copy.start()
    small[0].wait()
    small[1].wait()
    expand = (iota((16, 512), 1) // 32 == iota((16, 512), 0)).astype(BF16)
    w = lax.dot_general(weight_ref[...], expand, (((0,), (0,)), ((), ())), preferred_element_type=F32)
    diff = iota((40, 512), 0) - iota((40, 512), 1) % 32
    blocks = []
    for a in range(3):
        for e in range(3):
            block = jnp.zeros((40, 512), F32)
            for b in range(3):
                row = w[9 * a + 3 * b + e : 9 * a + 3 * b + e + 1, :]
                block = jnp.where(diff == b, row, block)
            blocks.append(block)
    matrix = jnp.concatenate(blocks, axis=0).astype(BF16)
    for f in range(4):
        width = width_ref[f]
        mats_ref[f, :512], mats_ref[f, 512:1024] = column_matrices(width)
        mats_ref[f, 1024:1072, :192] = row_matrix(48, 64, 15, width)
        mats_ref[f, 1072:, :120] = row_matrix(64, 40, -15, width)
    for f in range(4):
        copies[f].wait()
        terms = dot(matrix, held[f].reshape(512, 1024))
        for a in range(3):
            part = terms[120 * a : 120 * a + 120]
            if f == 0 or a == 2:
                acc_ref[f + a] = part
            else:
                acc_ref[f + a] += part
    for p in range(6):
        full = acc_ref[p]
        out_ref[p] = shift_cols(full[0:40], 1) + full[40:80] + shift_cols(full[80:120], -1)


def back_project(half_width, conv_weight, out_cotangent):
    return pl.pallas_call(
        back_kernel,
        out_shape=(
            jax.ShapeDtypeStruct((6, 40, 1024), F32),
            jax.ShapeDtypeStruct((4, 1136, 256), BF16),
            jax.ShapeDtypeStruct((4, 16, 32, 1024), BF16),
        ),
        in_specs=[hbm(), hbm(), hbm()],
        out_specs=(vmem(),) * 3,
        scratch_shapes=[
            pltpu.VMEM((6, 120, 1024), F32),
            pltpu.VMEM((16, 27), BF16),
            pltpu.SMEM((4,), jnp.int32),
            pltpu.SemaphoreType.DMA((6,)),
        ],
        compiler_params=params(),
        cost_estimate=pl.CostEstimate(flops=3 * 10**9, bytes_accessed=7 * 2**20, transcendentals=10**5),
        name="back_project",
    )(half_width, conv_weight, out_cotangent)


def beam_kernel(mats_ref, sky_ref, b_ref, a_ref, grad_ref, beam_ref, core_ref, far_ref):
    even = lax.axis_index("sky") % 2 == 0
    f_even = lax.axis_index("freq") % 2 == 0
    row = iota((48, 1024), 0)
    first = jnp.where(lax.axis_index("sky") == 0, 1, 0)
    last = jnp.where(lax.axis_index("sky") == lax.axis_size("sky") - 1, 33, 34)
    keep = (row >= first) & (row < last)
    smooth = []
    for f in range(4):
        ra, rb = a_ref[f], b_ref[f]
        above = jnp.where(even, rb, ra)
        below = jnp.where(even, ra, rb)
        rows = jnp.concatenate([above, sky_ref[f], below], axis=0)
        smooth.append(three_parts(blur_columns(rows, mats_ref[f, :512], mats_ref[f, 512:1024])))
    beams = [jnp.where(keep, dot(mats_ref[f, 1024:1072, :192], smooth[f]), 0.0) for f in range(4)]
    for f in range(4):
        beam_ref[f] = beams[f].astype(BF16)
    edges = []
    for f, p in ((0, 0), (3, 5)):
        g = grad_ref[p]
        edges.append(jnp.concatenate([beams[f][:40], g], axis=0))
    core_ref[...] = jnp.where(f_even, edges[1], edges[0]).astype(BF16)
    far_ref[...] = jnp.where(f_even, edges[0], edges[1]).astype(BF16)


def beam_of(mats, sky_cube, from_b, from_a, grad):
    edge = jax.ShapeDtypeStruct((80, 1024), BF16)
    return pl.pallas_call(
        beam_kernel,
        out_shape=(jax.ShapeDtypeStruct((4, 48, 1024), BF16), edge, edge),
        in_specs=[vmem()] * 5,
        out_specs=(vmem(), vmem(), vmem()),
        compiler_params=params(),
        cost_estimate=pl.CostEstimate(flops=10**9, bytes_accessed=4 * 2**20, transcendentals=0),
        name="beam",
    )(mats, sky_cube, from_b, from_a, grad)


def three_shifts(beam):
    wide = beam[:40].astype(F32)
    parts = [shift_cols(wide, e - 1) for e in range(3)] + [jnp.zeros((8, beam.shape[1]), F32)]
    return jnp.concatenate(parts, axis=0).astype(BF16)


def contract(a, b):
    return lax.dot_general(a, b, (((1,), (1,)), ((), ())), preferred_element_type=F32)


def pick_taps(gram, step):
    n = gram.shape[1]
    col = iota((4, 8, n), 2) % 128
    diff = col - 40 * (col // 40) - (iota((4, 8, n), 0) * 8 + iota((4, 8, n), 1))
    tiles = gram.reshape(16, 4, 8, n)
    parts = [jnp.where((diff == b)[None], tiles, 0.0).sum(axis=1) for b in range(3)]
    sums = jnp.concatenate(parts, axis=2).reshape(128, 3 * n)
    top = sums.astype(BF16)
    rest = sums - top.astype(F32)
    mid = rest.astype(BF16)
    low = (rest - mid.astype(F32)).astype(BF16)
    i = iota((3 * n, 128), 0)
    b, a, e = i // n, step * (i % n // 128), i % 128 // 40
    chosen = (iota((3 * n, 128), 1) % 32 == jnp.where(e < 3, 9 * a + 3 * b + e, 99)).astype(F32).astype(BF16)
    total = dot(top, chosen) + (dot(mid, chosen) + dot(low, chosen))
    return total.reshape(16, 8, 128).sum(axis=1)


def inner_kernel(beam_ref, cot_ref, out_ref, shift_ref, gram_ref):
    for p in range(4):
        shift_ref[pl.ds(128 * p, 128)] = three_shifts(beam_ref[p])
    for f in (1, 0, 2, 3):
        low, high = max(f - 1, 0), min(f + 2, 4)
        terms = contract(cot_ref[f].reshape(512, 1024), shift_ref[pl.ds(128 * low, 128 * (high - low))])
        cols = pl.ds(128 * (low - f + 1), 128 * (high - low))
        if f == 1:
            gram_ref[:, cols] = terms
        else:
            gram_ref[:, cols] += terms
    out_ref[...] = pick_taps(gram_ref[...], 1)


def inner_terms(beam, out_cotangent):
    return pl.pallas_call(
        inner_kernel,
        out_shape=jax.ShapeDtypeStruct((16, 128), F32),
        in_specs=[vmem(), vmem()],
        out_specs=vmem(),
        scratch_shapes=[pltpu.VMEM((512, 1024), BF16), pltpu.VMEM((512, 384), F32)],
        compiler_params=params(),
        cost_estimate=pl.CostEstimate(flops=2 * 10**9, bytes_accessed=6 * 2**20, transcendentals=0),
        name="inner_terms",
    )(beam, out_cotangent)


def outer_kernel(inner_ref, core_ref, far_ref, cot_ref, out_ref):
    even = lax.axis_index("freq") % 2 == 0
    core, far = core_ref[:40], far_ref[:40]
    before = three_shifts(jnp.where(even, far, core))
    after = three_shifts(jnp.where(even, core, far))
    low = contract(cot_ref[0].reshape(512, 1024), before)
    high = contract(cot_ref[3].reshape(512, 1024), after)
    total = inner_ref[...] + pick_taps(jnp.concatenate([low, high], axis=1), 2)
    placed = jnp.where(iota((16, 128), 1) // 32 == iota((16, 128), 0) % 4, total, 0.0)
    packed = placed.reshape(4, 4, 128).sum(axis=1)
    out_ref[...] = jnp.broadcast_to(packed[None], out_ref.shape)


def outer_terms(inner, from_core, from_far, out_cotangent, copies):
    return pl.pallas_call(
        outer_kernel,
        out_shape=jax.ShapeDtypeStruct((copies, 4, 128), F32),
        in_specs=[vmem()] * 4,
        out_specs=vmem(),
        compiler_params=params(),
        cost_estimate=pl.CostEstimate(flops=5 * 10**8, bytes_accessed=3 * 2**20, transcendentals=0),
        name="outer_terms",
    )(inner, from_core, from_far, out_cotangent)


def spread_kernel(mats_ref, grad_ref, core_ref, far_ref, own_ref, to_a_ref, to_b_ref):
    s_even = lax.axis_index("sky") % 2 == 0
    even = lax.axis_index("freq") % 2 == 0
    core = core_ref[40:].astype(F32)
    far = far_ref[40:].astype(F32)
    row = iota((40, 1024), 0)
    first = jnp.where(lax.axis_index("sky") == 0, 1, 0)
    last = jnp.where(lax.axis_index("sky") == lax.axis_size("sky") - 1, 33, 34)
    keep = (row >= first) & (row < last)
    shared = (row < 2) | (row >= 32)
    smooth = []
    for f in range(4):
        grad = grad_ref[f + 1]
        if f == 0:
            grad = grad + jnp.where(even, far, core)
        if f == 3:
            grad = grad + jnp.where(even, core, far)
        grad = jnp.where(keep, grad, 0.0)
        hi = grad.astype(BF16).astype(F32)
        lo = jnp.where(shared, grad - hi, 0.0)
        both = blur_columns(jnp.concatenate([hi, lo], axis=0).astype(BF16), mats_ref[f, :512], mats_ref[f, 512:1024])
        smooth.append(three_parts(both[:40] + both[40:]))
    for f in range(4):
        out = dot(mats_ref[f, 1072:, :120], smooth[f])
        own_ref[f] = out[16:48]
        to_a_ref[f] = jnp.where(s_even, out[48:], out[:16]).astype(BF16)
        to_b_ref[f] = jnp.where(s_even, out[:16], out[48:]).astype(BF16)


def spread(mats, grad, from_core, from_far):
    edge = jax.ShapeDtypeStruct((4, HALF, 1024), BF16)
    return pl.pallas_call(
        spread_kernel,
        out_shape=(jax.ShapeDtypeStruct((4, 32, 1024), F32), edge, edge),
        in_specs=[vmem()] * 4,
        out_specs=(vmem(), vmem(), vmem()),
        compiler_params=params(),
        cost_estimate=pl.CostEstimate(flops=10**9, bytes_accessed=3 * 2**20, transcendentals=0),
        name="spread",
    )(mats, grad, from_core, from_far)


def final_kernel(scale, own_ref, a_ref, b_ref, terms_ref, sky_ref, grad_ref):
    even = lax.axis_index("sky") % 2 == 0
    for f in range(4):
        ra, rb = a_ref[f], b_ref[f]
        sky_ref[f, :HALF] = own_ref[f, :HALF] + jnp.where(even, rb, ra).astype(F32)
        sky_ref[f, HALF:] = own_ref[f, HALF:] + jnp.where(even, ra, rb).astype(F32)
    packed = jnp.sum(terms_ref[...], axis=0) * scale
    rows = jnp.broadcast_to(packed[:, None, :], (4, 4, 128)).reshape(16, 128)
    placed = jnp.where(iota((16, 128), 1) // 32 == iota((16, 128), 0) % 4, rows, 0.0)
    fold = (iota((128, 128), 0) % 32 == iota((128, 128), 1)).astype(F32)
    out = jnp.dot(placed, fold, preferred_element_type=F32, precision=lax.Precision.HIGHEST)
    grad_ref[...] = out[:, :27]


def finish(scale, own, from_a, from_b, terms):
    def body(*refs):
        final_kernel(scale, *refs)

    return pl.pallas_call(
        body,
        out_shape=(jax.ShapeDtypeStruct((4, 32, 1024), F32), jax.ShapeDtypeStruct((16, 27), F32)),
        in_specs=[vmem()] * 4,
        out_specs=(vmem(), vmem()),
        compiler_params=params(),
        cost_estimate=pl.CostEstimate(flops=10**6, bytes_accessed=2 * 2**20, transcendentals=0),
        name="finish",
    )(own, from_a, from_b, terms)


def pair_swap(x, axis, odd_pairs):
    size = lax.axis_size(axis)
    first = 1 if odd_pairs else 0
    pairs = [(i, i + 1) for i in range(first, size - 1, 2)]
    return lax.ppermute(x, axis, pairs + [(j, i) for i, j in pairs])


def per_device(sky_cube, half_width, conv_weight, out_cotangent):
    freq_count, row_count, length = sky_cube.shape
    s_even = lax.axis_index("sky") % 2 == 0
    out_cotangent, conv_weight, half_width = (
        pltpu.with_memory_space_constraint(x, pltpu.HBM) for x in (out_cotangent, conv_weight, half_width)
    )

    half = lax.axis_index("sky") % 2
    for_a = lax.dynamic_slice_in_dim(sky_cube, HALF - HALF * half, HALF, 1)
    for_b = lax.dynamic_slice_in_dim(sky_cube, HALF * half, HALF, 1)
    sky_a, sky_b = pair_swap(for_a, "sky", False), pair_swap(for_b, "sky", True)
    grad, mats, held = back_project(half_width, conv_weight, out_cotangent)
    beam, to_core, to_far = beam_of(mats, sky_cube, sky_b, sky_a, grad)
    from_core, from_far = pair_swap(to_core, "freq", False), pair_swap(to_far, "freq", True)
    inner = inner_terms(beam, held)
    own, to_a, to_b = spread(mats, grad, from_core, from_far)
    own, to_a, to_b, inner = lax.optimization_barrier((own, to_a, to_b, inner))
    copies = lax.axis_size("freq") * lax.axis_size("sky")
    terms = outer_terms(inner, from_core, from_far, held, copies)
    to_a, to_b, terms = lax.optimization_barrier((to_a, to_b, terms))
    gathered = lax.all_to_all(terms, ("freq", "sky"), 0, 0)
    row_a, row_b = pair_swap(to_a, "sky", False), pair_swap(to_b, "sky", True)
    cell_count = freq_count * lax.axis_size("freq") * row_count * lax.axis_size("sky") * length
    return finish(1.0 / math.sqrt(cell_count), own, row_a, row_b, gathered)


def solution(mesh):
    return jax.shard_map(
        per_device,
        mesh=mesh,
        in_specs=(P("freq", "sky", None), P("freq"), P(), P(None, "freq", "sky", None)),
        out_specs=(P("freq", "sky", None), P()),
        check_vma=False,
    )
```

```python
import math

import jax
import jax.numpy as jnp
from jax import lax
from jax.experimental import pallas as pl
from jax.experimental.pallas import tpu as pltpu
from jax.sharding import PartitionSpec as P

MAXH = 12
HALF = 16
F32 = jnp.float32
BF16 = jnp.bfloat16
MIB = 1024 * 1024


def params(mib=24):
    return pltpu.CompilerParams(vmem_limit_bytes=mib * MIB)


def iota(shape, dim):
    return lax.broadcasted_iota(jnp.int32, shape, dim)


def dot(a, b):
    return jnp.dot(a, b, preferred_element_type=F32)


def split(x):
    hi = x.astype(BF16)
    return hi, (x - hi.astype(F32)).astype(BF16)


def taps_at(offsets, width):
    def profile(d):
        w = jnp.full(d.shape, width, jnp.int32)
        wf = w.astype(F32)
        df = d.astype(F32)
        return jnp.where(jnp.abs(d) <= w, jnp.exp(-2.0 * (df * df) / (wf * wf)), 0.0)

    line = profile(iota((8, 128), 1) - 64)
    norm = jnp.sqrt(jnp.sum(line * line, axis=1, keepdims=True))[:1]
    return profile(offsets) / norm


def column_matrices(width):
    band = taps_at(iota((160, 128), 0) - 16 - iota((160, 128), 1), width)
    left = jnp.concatenate([jnp.zeros((112, 128), F32), band, jnp.zeros((240, 128), F32)], axis=0)
    right = jnp.concatenate([jnp.zeros((240, 128), F32), band, jnp.zeros((112, 128), F32)], axis=0)
    return split(jnp.concatenate([left, right], axis=1))


def blur_columns(rows, hi, lo):
    n = rows.shape[0]
    edge = jnp.zeros((n, 128), BF16)
    padded = jnp.concatenate([edge, rows, edge], axis=1)
    stacked = jnp.concatenate([padded[:, 256 * j : 256 * j + 512] for j in range(4)], axis=0)
    out = dot(stacked, hi) + dot(stacked, lo)
    return jnp.concatenate([out[n * j : n * j + n] for j in range(4)], axis=1)


def row_matrix(count, n, base, width):
    hi, lo = split(taps_at(iota((count, n), 1) - iota((count, n), 0) - base, width))
    hi, lo = hi.astype(F32), lo.astype(F32)
    return jnp.concatenate([hi, hi, lo], axis=1).astype(BF16)


def three_parts(source):
    hi = source.astype(BF16).astype(F32)
    return jnp.concatenate([hi, source - hi, hi], axis=0).astype(BF16)


def shift_cols(x, offset):
    if offset == 0:
        return x
    length = x.shape[-1]
    col = iota(x.shape, x.ndim - 1)
    if offset > 0:
        return jnp.where(col < length - 1, pltpu.roll(x, length - 1, x.ndim - 1), 0.0)
    return jnp.where(col > 0, pltpu.roll(x, 1, x.ndim - 1), 0.0)


def vmem():
    return pl.BlockSpec(memory_space=pltpu.VMEM)


def hbm():
    return pl.BlockSpec(memory_space=pltpu.HBM)


def plane_copies(cot_ref, planes, held, sem):
    return [pltpu.make_async_copy(cot_ref.at[:, f], held.at[i], sem.at[i]) for i, f in enumerate(planes)]


def back_kernel(
    width_hbm, weight_hbm, cot_ref, out_ref, mats_ref, held, acc_ref, weight_ref, width_ref, sem
):
    small = [
        pltpu.make_async_copy(weight_hbm, weight_ref, sem.at[4]),
        pltpu.make_async_copy(width_hbm, width_ref, sem.at[5]),
    ]
    for copy in small:
        copy.start()
    copies = plane_copies(cot_ref, range(4), held, sem)
    for copy in copies:
        copy.start()
    small[0].wait()
    small[1].wait()
    expand = (iota((16, 512), 1) // 32 == iota((16, 512), 0)).astype(BF16)
    w = lax.dot_general(weight_ref[...], expand, (((0,), (0,)), ((), ())), preferred_element_type=F32)
    diff = iota((40, 512), 0) - iota((40, 512), 1) % 32
    blocks = []
    for a in range(3):
        for e in range(3):
            block = jnp.zeros((40, 512), F32)
            for b in range(3):
                row = w[9 * a + 3 * b + e : 9 * a + 3 * b + e + 1, :]
                block = jnp.where(diff == b, row, block)
            blocks.append(block)
    matrix = jnp.concatenate(blocks, axis=0).astype(BF16)
    for f in range(4):
        width = width_ref[f]
        mats_ref[f, :512], mats_ref[f, 512:1024] = column_matrices(width)
        mats_ref[f, 1024:1072, :192] = row_matrix(48, 64, 15, width)
        mats_ref[f, 1072:, :120] = row_matrix(64, 40, -15, width)
    for f in range(4):
        copies[f].wait()
        terms = dot(matrix, held[f].reshape(512, 1024))
        for a in range(3):
            part = terms[120 * a : 120 * a + 120]
            if f == 0 or a == 2:
                acc_ref[f + a] = part
            else:
                acc_ref[f + a] += part
    for p in range(6):
        full = acc_ref[p]
        out_ref[p] = shift_cols(full[0:40], 1) + full[40:80] + shift_cols(full[80:120], -1)


def back_project(half_width, conv_weight, out_cotangent):
    return pl.pallas_call(
        back_kernel,
        out_shape=(
            jax.ShapeDtypeStruct((6, 40, 1024), F32),
            jax.ShapeDtypeStruct((4, 1136, 256), BF16),
            jax.ShapeDtypeStruct((4, 16, 32, 1024), BF16),
        ),
        in_specs=[hbm(), hbm(), hbm()],
        out_specs=(vmem(),) * 3,
        scratch_shapes=[
            pltpu.VMEM((6, 120, 1024), F32),
            pltpu.VMEM((16, 27), BF16),
            pltpu.SMEM((4,), jnp.int32),
            pltpu.SemaphoreType.DMA((6,)),
        ],
        compiler_params=params(),
        cost_estimate=pl.CostEstimate(flops=3 * 10**9, bytes_accessed=7 * 2**20, transcendentals=10**5),
        name="back_project",
    )(half_width, conv_weight, out_cotangent)


def beam_kernel(mats_ref, sky_ref, b_ref, a_ref, grad_ref, beam_ref, core_ref, far_ref):
    even = lax.axis_index("sky") % 2 == 0
    f_even = lax.axis_index("freq") % 2 == 0
    row = iota((48, 1024), 0)
    first = jnp.where(lax.axis_index("sky") == 0, 1, 0)
    last = jnp.where(lax.axis_index("sky") == lax.axis_size("sky") - 1, 33, 34)
    keep = (row >= first) & (row < last)
    smooth = []
    for f in range(4):
        ra, rb = a_ref[f], b_ref[f]
        above = jnp.where(even, rb, ra)
        below = jnp.where(even, ra, rb)
        rows = jnp.concatenate([above, sky_ref[f], below], axis=0)
        smooth.append(three_parts(blur_columns(rows, mats_ref[f, :512], mats_ref[f, 512:1024])))
    beams = [jnp.where(keep, dot(mats_ref[f, 1024:1072, :192], smooth[f]), 0.0) for f in range(4)]
    for f in range(4):
        beam_ref[f] = beams[f].astype(BF16)
    edges = []
    for f, p in ((0, 0), (3, 5)):
        g = grad_ref[p]
        edges.append(jnp.concatenate([beams[f][:40], g], axis=0))
    core_ref[...] = jnp.where(f_even, edges[1], edges[0]).astype(BF16)
    far_ref[...] = jnp.where(f_even, edges[0], edges[1]).astype(BF16)


def beam_of(mats, sky_cube, from_b, from_a, grad):
    edge = jax.ShapeDtypeStruct((80, 1024), BF16)
    return pl.pallas_call(
        beam_kernel,
        out_shape=(jax.ShapeDtypeStruct((4, 48, 1024), BF16), edge, edge),
        in_specs=[vmem()] * 5,
        out_specs=(vmem(), vmem(), vmem()),
        compiler_params=params(),
        cost_estimate=pl.CostEstimate(flops=10**9, bytes_accessed=4 * 2**20, transcendentals=0),
        name="beam",
    )(mats, sky_cube, from_b, from_a, grad)


def three_shifts(beam):
    wide = beam[:40].astype(F32)
    parts = [shift_cols(wide, e - 1) for e in range(3)] + [jnp.zeros((8, beam.shape[1]), F32)]
    return jnp.concatenate(parts, axis=0).astype(BF16)


def contract(a, b):
    return lax.dot_general(a, b, (((1,), (1,)), ((), ())), preferred_element_type=F32)


def pick_taps(gram, step):
    n = gram.shape[1]
    col = iota((4, 8, n), 2) % 128
    diff = col - 40 * (col // 40) - (iota((4, 8, n), 0) * 8 + iota((4, 8, n), 1))
    tiles = gram.reshape(16, 4, 8, n)
    parts = [jnp.where((diff == b)[None], tiles, 0.0).sum(axis=1) for b in range(3)]
    sums = jnp.concatenate(parts, axis=2).reshape(128, 3 * n)
    top = sums.astype(BF16)
    rest = sums - top.astype(F32)
    mid = rest.astype(BF16)
    low = (rest - mid.astype(F32)).astype(BF16)
    i = iota((3 * n, 128), 0)
    b, a, e = i // n, step * (i % n // 128), i % 128 // 40
    chosen = (iota((3 * n, 128), 1) % 32 == jnp.where(e < 3, 9 * a + 3 * b + e, 99)).astype(F32).astype(BF16)
    total = dot(top, chosen) + (dot(mid, chosen) + dot(low, chosen))
    return total.reshape(16, 8, 128).sum(axis=1)


def inner_kernel(beam_ref, cot_ref, out_ref, shift_ref, gram_ref):
    for p in range(4):
        shift_ref[pl.ds(128 * p, 128)] = three_shifts(beam_ref[p])
    for f in (1, 0, 2, 3):
        low, high = max(f - 1, 0), min(f + 2, 4)
        terms = contract(cot_ref[f].reshape(512, 1024), shift_ref[pl.ds(128 * low, 128 * (high - low))])
        cols = pl.ds(128 * (low - f + 1), 128 * (high - low))
        if f == 1:
            gram_ref[:, cols] = terms
        else:
            gram_ref[:, cols] += terms
    out_ref[...] = pick_taps(gram_ref[...], 1)


def inner_terms(beam, out_cotangent):
    return pl.pallas_call(
        inner_kernel,
        out_shape=jax.ShapeDtypeStruct((16, 128), F32),
        in_specs=[vmem(), vmem()],
        out_specs=vmem(),
        scratch_shapes=[pltpu.VMEM((512, 1024), BF16), pltpu.VMEM((512, 384), F32)],
        compiler_params=params(),
        cost_estimate=pl.CostEstimate(flops=2 * 10**9, bytes_accessed=6 * 2**20, transcendentals=0),
        name="inner_terms",
    )(beam, out_cotangent)


def outer_kernel(inner_ref, core_ref, far_ref, cot_ref, out_ref):
    even = lax.axis_index("freq") % 2 == 0
    core, far = core_ref[:40], far_ref[:40]
    before = three_shifts(jnp.where(even, far, core))
    after = three_shifts(jnp.where(even, core, far))
    low = contract(cot_ref[0].reshape(512, 1024), before)
    high = contract(cot_ref[3].reshape(512, 1024), after)
    total = inner_ref[...] + pick_taps(jnp.concatenate([low, high], axis=1), 2)
    placed = jnp.where(iota((16, 128), 1) // 32 == iota((16, 128), 0) % 4, total, 0.0)
    packed = placed.reshape(4, 4, 128).sum(axis=1)
    out_ref[...] = jnp.broadcast_to(packed[None], out_ref.shape)


def spread_kernel(mats_ref, grad_ref, core_ref, far_ref, own_ref, to_a_ref, to_b_ref):
    s_even = lax.axis_index("sky") % 2 == 0
    even = lax.axis_index("freq") % 2 == 0
    core = core_ref[40:].astype(F32)
    far = far_ref[40:].astype(F32)
    row = iota((40, 1024), 0)
    first = jnp.where(lax.axis_index("sky") == 0, 1, 0)
    last = jnp.where(lax.axis_index("sky") == lax.axis_size("sky") - 1, 33, 34)
    keep = (row >= first) & (row < last)
    shared = (row < 2) | (row >= 32)
    smooth = []
    for f in range(4):
        grad = grad_ref[f + 1]
        if f == 0:
            grad = grad + jnp.where(even, far, core)
        if f == 3:
            grad = grad + jnp.where(even, core, far)
        grad = jnp.where(keep, grad, 0.0)
        hi = grad.astype(BF16).astype(F32)
        lo = jnp.where(shared, grad - hi, 0.0)
        both = blur_columns(jnp.concatenate([hi, lo], axis=0).astype(BF16), mats_ref[f, :512], mats_ref[f, 512:1024])
        smooth.append(three_parts(both[:40] + both[40:]))
    for f in range(4):
        out = dot(mats_ref[f, 1072:, :120], smooth[f])
        own_ref[f] = out[16:48]
        to_a_ref[f] = jnp.where(s_even, out[48:], out[:16]).astype(BF16)
        to_b_ref[f] = jnp.where(s_even, out[:16], out[48:]).astype(BF16)


def spread_and_outer(mats, grad, from_core, from_far, inner, held, copies):
    def body(mats_ref, grad_ref, core_ref, far_ref, inner_ref, cot_ref, own_ref, to_a_ref, to_b_ref, terms_ref):
        outer_kernel(inner_ref, core_ref, far_ref, cot_ref, terms_ref)
        spread_kernel(mats_ref, grad_ref, core_ref, far_ref, own_ref, to_a_ref, to_b_ref)

    edge = jax.ShapeDtypeStruct((4, HALF, 1024), BF16)
    terms = jax.ShapeDtypeStruct((copies, 4, 128), F32)
    return pl.pallas_call(
        body,
        out_shape=(jax.ShapeDtypeStruct((4, 32, 1024), F32), edge, edge, terms),
        in_specs=[vmem()] * 6,
        out_specs=(vmem(),) * 4,
        compiler_params=params(),
        cost_estimate=pl.CostEstimate(flops=15 * 10**8, bytes_accessed=6 * 2**20, transcendentals=0),
        name="spread_and_outer",
    )(mats, grad, from_core, from_far, inner, held)


def final_kernel(scale, own_ref, a_ref, b_ref, terms_ref, sky_ref, grad_ref):
    even = lax.axis_index("sky") % 2 == 0
    for f in range(4):
        ra, rb = a_ref[f], b_ref[f]
        sky_ref[f, :HALF] = own_ref[f, :HALF] + jnp.where(even, rb, ra).astype(F32)
        sky_ref[f, HALF:] = own_ref[f, HALF:] + jnp.where(even, ra, rb).astype(F32)
    packed = jnp.sum(terms_ref[...], axis=0) * scale
    rows = jnp.broadcast_to(packed[:, None, :], (4, 4, 128)).reshape(16, 128)
    placed = jnp.where(iota((16, 128), 1) // 32 == iota((16, 128), 0) % 4, rows, 0.0)
    fold = (iota((128, 128), 0) % 32 == iota((128, 128), 1)).astype(F32)
    out = jnp.dot(placed, fold, preferred_element_type=F32, precision=lax.Precision.HIGHEST)
    grad_ref[...] = out[:, :27]


def finish(scale, own, from_a, from_b, terms):
    def body(*refs):
        final_kernel(scale, *refs)

    return pl.pallas_call(
        body,
        out_shape=(jax.ShapeDtypeStruct((4, 32, 1024), F32), jax.ShapeDtypeStruct((16, 27), F32)),
        in_specs=[vmem()] * 4,
        out_specs=(vmem(), vmem()),
        compiler_params=params(),
        cost_estimate=pl.CostEstimate(flops=10**6, bytes_accessed=2 * 2**20, transcendentals=0),
        name="finish",
    )(own, from_a, from_b, terms)


def pair_swap(x, axis, odd_pairs):
    size = lax.axis_size(axis)
    first = 1 if odd_pairs else 0
    pairs = [(i, i + 1) for i in range(first, size - 1, 2)]
    return lax.ppermute(x, axis, pairs + [(j, i) for i, j in pairs])


def per_device(sky_cube, half_width, conv_weight, out_cotangent):
    freq_count, row_count, length = sky_cube.shape
    s_even = lax.axis_index("sky") % 2 == 0
    out_cotangent, conv_weight, half_width = (
        pltpu.with_memory_space_constraint(x, pltpu.HBM) for x in (out_cotangent, conv_weight, half_width)
    )

    half = lax.axis_index("sky") % 2
    for_a = lax.dynamic_slice_in_dim(sky_cube, HALF - HALF * half, HALF, 1)
    for_b = lax.dynamic_slice_in_dim(sky_cube, HALF * half, HALF, 1)
    sky_a, sky_b = pair_swap(for_a, "sky", False), pair_swap(for_b, "sky", True)
    grad, mats, held = back_project(half_width, conv_weight, out_cotangent)
    beam, to_core, to_far = beam_of(mats, sky_cube, sky_b, sky_a, grad)
    from_core, from_far = pair_swap(to_core, "freq", False), pair_swap(to_far, "freq", True)
    inner = inner_terms(beam, held)
    copies = lax.axis_size("freq") * lax.axis_size("sky")
    own, to_a, to_b, terms = spread_and_outer(mats, grad, from_core, from_far, inner, held, copies)
    gathered = lax.all_to_all(terms, ("freq", "sky"), 0, 0)
    row_a, row_b = pair_swap(to_a, "sky", False), pair_swap(to_b, "sky", True)
    cell_count = freq_count * lax.axis_size("freq") * row_count * lax.axis_size("sky") * length
    return finish(1.0 / math.sqrt(cell_count), own, row_a, row_b, gathered)


def solution(mesh):
    return jax.shard_map(
        per_device,
        mesh=mesh,
        in_specs=(P("freq", "sky", None), P("freq"), P(), P(None, "freq", "sky", None)),
        out_specs=(P("freq", "sky", None), P()),
        check_vma=False,
    )
```

```python
import math

import jax
import jax.numpy as jnp
from jax import lax
from jax.experimental import pallas as pl
from jax.experimental.pallas import tpu as pltpu
from jax.sharding import PartitionSpec as P

MAXH = 12
HALF = 16
F32 = jnp.float32
BF16 = jnp.bfloat16
MIB = 1024 * 1024


def params(mib=24):
    return pltpu.CompilerParams(vmem_limit_bytes=mib * MIB)


def iota(shape, dim):
    return lax.broadcasted_iota(jnp.int32, shape, dim)


def dot(a, b):
    return jnp.dot(a, b, preferred_element_type=F32)


def split(x):
    hi = x.astype(BF16)
    return hi, (x - hi.astype(F32)).astype(BF16)


def taps_at(offsets, width):
    def profile(d):
        w = jnp.full(d.shape, width, jnp.int32)
        wf = w.astype(F32)
        df = d.astype(F32)
        return jnp.where(jnp.abs(d) <= w, jnp.exp(-2.0 * (df * df) / (wf * wf)), 0.0)

    line = profile(iota((8, 128), 1) - 64)
    norm = jnp.sqrt(jnp.sum(line * line, axis=1, keepdims=True))[:1]
    return profile(offsets) / norm


def column_matrices(width):
    band = taps_at(iota((160, 128), 0) - 16 - iota((160, 128), 1), width)
    left = jnp.concatenate([jnp.zeros((112, 128), F32), band, jnp.zeros((240, 128), F32)], axis=0)
    right = jnp.concatenate([jnp.zeros((240, 128), F32), band, jnp.zeros((112, 128), F32)], axis=0)
    return split(jnp.concatenate([left, right], axis=1))


def blur_columns(rows, hi, lo):
    n = rows.shape[0]
    edge = jnp.zeros((n, 128), BF16)
    padded = jnp.concatenate([edge, rows, edge], axis=1)
    stacked = jnp.concatenate([padded[:, 256 * j : 256 * j + 512] for j in range(4)], axis=0)
    out = dot(stacked, hi) + dot(stacked, lo)
    return jnp.concatenate([out[n * j : n * j + n] for j in range(4)], axis=1)


def row_matrix(count, n, base, width):
    hi, lo = split(taps_at(iota((count, n), 1) - iota((count, n), 0) - base, width))
    hi, lo = hi.astype(F32), lo.astype(F32)
    return jnp.concatenate([hi, hi, lo], axis=1).astype(BF16)


def three_parts(source):
    hi = source.astype(BF16).astype(F32)
    return jnp.concatenate([hi, source - hi, hi], axis=0).astype(BF16)


def shift_cols(x, offset):
    if offset == 0:
        return x
    length = x.shape[-1]
    col = iota(x.shape, x.ndim - 1)
    if offset > 0:
        return jnp.where(col < length - 1, pltpu.roll(x, length - 1, x.ndim - 1), 0.0)
    return jnp.where(col > 0, pltpu.roll(x, 1, x.ndim - 1), 0.0)


def vmem():
    return pl.BlockSpec(memory_space=pltpu.VMEM)


def hbm():
    return pl.BlockSpec(memory_space=pltpu.HBM)


def plane_copies(cot_ref, planes, held, sem):
    return [pltpu.make_async_copy(cot_ref.at[:, f], held.at[i], sem.at[i]) for i, f in enumerate(planes)]


def back_kernel(
    width_hbm, weight_hbm, cot_ref, out_ref, mats_ref, held, acc_ref, weight_ref, width_ref, sem
):
    small = [
        pltpu.make_async_copy(weight_hbm, weight_ref, sem.at[4]),
        pltpu.make_async_copy(width_hbm, width_ref, sem.at[5]),
    ]
    for copy in small:
        copy.start()
    copies = plane_copies(cot_ref, range(4), held, sem)
    for copy in copies:
        copy.start()
    small[0].wait()
    small[1].wait()
    expand = (iota((16, 512), 1) // 32 == iota((16, 512), 0)).astype(BF16)
    w = lax.dot_general(weight_ref[...], expand, (((0,), (0,)), ((), ())), preferred_element_type=F32)
    diff = iota((40, 512), 0) - iota((40, 512), 1) % 32
    blocks = []
    for a in range(3):
        for e in range(3):
            block = jnp.zeros((40, 512), F32)
            for b in range(3):
                row = w[9 * a + 3 * b + e : 9 * a + 3 * b + e + 1, :]
                block = jnp.where(diff == b, row, block)
            blocks.append(block)
    matrix = jnp.concatenate(blocks, axis=0).astype(BF16)
    for f in range(4):
        width = width_ref[f]
        mats_ref[f, :512], mats_ref[f, 512:1024] = column_matrices(width)
        mats_ref[f, 1024:1072, :192] = row_matrix(48, 64, 15, width)
        mats_ref[f, 1072:, :120] = row_matrix(64, 40, -15, width)
    for f in range(4):
        copies[f].wait()
        terms = dot(matrix, held[f].reshape(512, 1024))
        for a in range(3):
            part = terms[120 * a : 120 * a + 120]
            if f == 0 or a == 2:
                acc_ref[f + a] = part
            else:
                acc_ref[f + a] += part
    for p in range(6):
        full = acc_ref[p]
        out_ref[p] = shift_cols(full[0:40], 1) + full[40:80] + shift_cols(full[80:120], -1)


def back_project(half_width, conv_weight, out_cotangent):
    return pl.pallas_call(
        back_kernel,
        out_shape=(
            jax.ShapeDtypeStruct((6, 40, 1024), F32),
            jax.ShapeDtypeStruct((4, 1136, 256), BF16),
            jax.ShapeDtypeStruct((4, 16, 32, 1024), BF16),
        ),
        in_specs=[hbm(), hbm(), hbm()],
        out_specs=(vmem(),) * 3,
        scratch_shapes=[
            pltpu.VMEM((6, 120, 1024), F32),
            pltpu.VMEM((16, 27), BF16),
            pltpu.SMEM((4,), jnp.int32),
            pltpu.SemaphoreType.DMA((6,)),
        ],
        compiler_params=params(),
        cost_estimate=pl.CostEstimate(flops=3 * 10**9, bytes_accessed=7 * 2**20, transcendentals=10**5),
        name="back_project",
    )(half_width, conv_weight, out_cotangent)


def beam_kernel(mats_ref, sky_ref, b_ref, a_ref, grad_ref, beam_ref, core_ref, far_ref):
    even = lax.axis_index("sky") % 2 == 0
    f_even = lax.axis_index("freq") % 2 == 0
    row = iota((48, 1024), 0)
    first = jnp.where(lax.axis_index("sky") == 0, 1, 0)
    last = jnp.where(lax.axis_index("sky") == lax.axis_size("sky") - 1, 33, 34)
    keep = (row >= first) & (row < last)
    smooth = []
    for f in range(4):
        ra, rb = a_ref[f], b_ref[f]
        above = jnp.where(even, rb, ra)
        below = jnp.where(even, ra, rb)
        rows = jnp.concatenate([above, sky_ref[f], below], axis=0)
        smooth.append(three_parts(blur_columns(rows, mats_ref[f, :512], mats_ref[f, 512:1024])))
    beams = [jnp.where(keep, dot(mats_ref[f, 1024:1072, :192], smooth[f]), 0.0) for f in range(4)]
    for f in range(4):
        beam_ref[f] = beams[f].astype(BF16)
    edges = []
    for f, p in ((0, 0), (3, 5)):
        g = grad_ref[p]
        edges.append(jnp.concatenate([beams[f][:40], g], axis=0))
    core_ref[...] = jnp.where(f_even, edges[1], edges[0]).astype(BF16)
    far_ref[...] = jnp.where(f_even, edges[0], edges[1]).astype(BF16)


def beam_of(mats, sky_cube, from_b, from_a, grad):
    edge = jax.ShapeDtypeStruct((80, 1024), BF16)
    return pl.pallas_call(
        beam_kernel,
        out_shape=(jax.ShapeDtypeStruct((4, 48, 1024), BF16), edge, edge),
        in_specs=[vmem()] * 5,
        out_specs=(vmem(), vmem(), vmem()),
        compiler_params=params(),
        cost_estimate=pl.CostEstimate(flops=10**9, bytes_accessed=4 * 2**20, transcendentals=0),
        name="beam",
    )(mats, sky_cube, from_b, from_a, grad)


def three_shifts(beam):
    wide = beam[:40].astype(F32)
    parts = [shift_cols(wide, e - 1) for e in range(3)] + [jnp.zeros((8, beam.shape[1]), F32)]
    return jnp.concatenate(parts, axis=0).astype(BF16)


def contract(a, b):
    return lax.dot_general(a, b, (((1,), (1,)), ((), ())), preferred_element_type=F32)


def pick_taps(gram, step):
    n = gram.shape[1]
    col = iota((4, 8, n), 2) % 128
    diff = col - 40 * (col // 40) - (iota((4, 8, n), 0) * 8 + iota((4, 8, n), 1))
    tiles = gram.reshape(16, 4, 8, n)
    parts = [jnp.where((diff == b)[None], tiles, 0.0).sum(axis=1) for b in range(3)]
    sums = jnp.concatenate(parts, axis=2).reshape(128, 3 * n)
    top = sums.astype(BF16)
    rest = sums - top.astype(F32)
    mid = rest.astype(BF16)
    low = (rest - mid.astype(F32)).astype(BF16)
    i = iota((3 * n, 128), 0)
    b, a, e = i // n, step * (i % n // 128), i % 128 // 40
    chosen = (iota((3 * n, 128), 1) % 32 == jnp.where(e < 3, 9 * a + 3 * b + e, 99)).astype(F32).astype(BF16)
    total = dot(top, chosen) + (dot(mid, chosen) + dot(low, chosen))
    return total.reshape(16, 8, 128).sum(axis=1)


def inner_kernel(beam_ref, cot_ref, out_ref, shift_ref, gram_ref):
    for p in range(4):
        shift_ref[pl.ds(128 * p, 128)] = three_shifts(beam_ref[p])
    for f in (1, 0, 2, 3):
        low, high = max(f - 1, 0), min(f + 2, 4)
        terms = contract(cot_ref[f].reshape(512, 1024), shift_ref[pl.ds(128 * low, 128 * (high - low))])
        cols = pl.ds(128 * (low - f + 1), 128 * (high - low))
        if f == 1:
            gram_ref[:, cols] = terms
        else:
            gram_ref[:, cols] += terms
    out_ref[...] = pick_taps(gram_ref[...], 1)


def inner_terms(beam, out_cotangent):
    return pl.pallas_call(
        inner_kernel,
        out_shape=jax.ShapeDtypeStruct((16, 128), F32),
        in_specs=[vmem(), vmem()],
        out_specs=vmem(),
        scratch_shapes=[pltpu.VMEM((512, 1024), BF16), pltpu.VMEM((512, 384), F32)],
        compiler_params=params(),
        cost_estimate=pl.CostEstimate(flops=2 * 10**9, bytes_accessed=6 * 2**20, transcendentals=0),
        name="inner_terms",
    )(beam, out_cotangent)


def outer_kernel(inner_ref, core_ref, far_ref, cot_ref, out_ref):
    even = lax.axis_index("freq") % 2 == 0
    core, far = core_ref[:40], far_ref[:40]
    before = three_shifts(jnp.where(even, far, core))
    after = three_shifts(jnp.where(even, core, far))
    low = contract(cot_ref[0].reshape(512, 1024), before)
    high = contract(cot_ref[3].reshape(512, 1024), after)
    total = inner_ref[...] + pick_taps(jnp.concatenate([low, high], axis=1), 2)
    placed = jnp.where(iota((16, 128), 1) // 32 == iota((16, 128), 0) % 4, total, 0.0)
    packed = placed.reshape(4, 4, 128).sum(axis=1)
    out_ref[...] = jnp.broadcast_to(packed[None], out_ref.shape)


def spread_kernel(mats_ref, grad_ref, core_ref, far_ref, own_ref, to_a_ref, to_b_ref):
    s_even = lax.axis_index("sky") % 2 == 0
    even = lax.axis_index("freq") % 2 == 0
    core = core_ref[40:].astype(F32)
    far = far_ref[40:].astype(F32)
    row = iota((40, 1024), 0)
    first = jnp.where(lax.axis_index("sky") == 0, 1, 0)
    last = jnp.where(lax.axis_index("sky") == lax.axis_size("sky") - 1, 33, 34)
    keep = (row >= first) & (row < last)
    shared = (row < 2) | (row >= 32)
    smooth = []
    for f in range(4):
        grad = grad_ref[f + 1]
        if f == 0:
            grad = grad + jnp.where(even, far, core)
        if f == 3:
            grad = grad + jnp.where(even, core, far)
        grad = jnp.where(keep, grad, 0.0)
        hi = grad.astype(BF16).astype(F32)
        lo = jnp.where(shared, grad - hi, 0.0)
        both = blur_columns(jnp.concatenate([hi, lo], axis=0).astype(BF16), mats_ref[f, :512], mats_ref[f, 512:1024])
        smooth.append(three_parts(both[:40] + both[40:]))
    for f in range(4):
        out = dot(mats_ref[f, 1072:, :120], smooth[f])
        own_ref[f] = out[16:48]
        to_a_ref[f] = jnp.where(s_even, out[48:], out[:16]).astype(BF16)
        to_b_ref[f] = jnp.where(s_even, out[:16], out[48:]).astype(BF16)


def spread_and_outer(mats, grad, from_core, from_far, inner, held, copies):
    def body(mats_ref, grad_ref, core_ref, far_ref, inner_ref, cot_ref, own_ref, to_a_ref, to_b_ref, terms_ref):
        spread_kernel(mats_ref, grad_ref, core_ref, far_ref, own_ref, to_a_ref, to_b_ref)
        outer_kernel(inner_ref, core_ref, far_ref, cot_ref, terms_ref)

    edge = jax.ShapeDtypeStruct((4, HALF, 1024), BF16)
    terms = jax.ShapeDtypeStruct((copies, 4, 128), F32)
    return pl.pallas_call(
        body,
        out_shape=(jax.ShapeDtypeStruct((4, 32, 1024), F32), edge, edge, terms),
        in_specs=[vmem()] * 6,
        out_specs=(vmem(),) * 4,
        compiler_params=params(),
        cost_estimate=pl.CostEstimate(flops=15 * 10**8, bytes_accessed=6 * 2**20, transcendentals=0),
        name="spread_and_outer",
    )(mats, grad, from_core, from_far, inner, held)


def final_kernel(scale, own_ref, a_ref, b_ref, terms_ref, sky_ref, grad_ref):
    even = lax.axis_index("sky") % 2 == 0
    for f in range(4):
        ra, rb = a_ref[f], b_ref[f]
        sky_ref[f, :HALF] = own_ref[f, :HALF] + jnp.where(even, rb, ra).astype(F32)
        sky_ref[f, HALF:] = own_ref[f, HALF:] + jnp.where(even, ra, rb).astype(F32)
    packed = jnp.sum(terms_ref[...], axis=0) * scale
    rows = jnp.broadcast_to(packed[:, None, :], (4, 4, 128)).reshape(16, 128)
    placed = jnp.where(iota((16, 128), 1) // 32 == iota((16, 128), 0) % 4, rows, 0.0)
    fold = (iota((128, 128), 0) % 32 == iota((128, 128), 1)).astype(F32)
    out = jnp.dot(placed, fold, preferred_element_type=F32, precision=lax.Precision.HIGHEST)
    grad_ref[...] = out[:, :27]


def finish(scale, own, from_a, from_b, terms):
    def body(*refs):
        final_kernel(scale, *refs)

    return pl.pallas_call(
        body,
        out_shape=(jax.ShapeDtypeStruct((4, 32, 1024), F32), jax.ShapeDtypeStruct((16, 27), F32)),
        in_specs=[vmem()] * 4,
        out_specs=(vmem(), vmem()),
        compiler_params=params(),
        cost_estimate=pl.CostEstimate(flops=10**6, bytes_accessed=2 * 2**20, transcendentals=0),
        name="finish",
    )(own, from_a, from_b, terms)


def pair_swap(x, axis, odd_pairs):
    size = lax.axis_size(axis)
    first = 1 if odd_pairs else 0
    pairs = [(i, i + 1) for i in range(first, size - 1, 2)]
    return lax.ppermute(x, axis, pairs + [(j, i) for i, j in pairs])


def per_device(sky_cube, half_width, conv_weight, out_cotangent):
    freq_count, row_count, length = sky_cube.shape
    s_even = lax.axis_index("sky") % 2 == 0
    out_cotangent, conv_weight, half_width = (
        pltpu.with_memory_space_constraint(x, pltpu.HBM) for x in (out_cotangent, conv_weight, half_width)
    )

    half = lax.axis_index("sky") % 2
    for_a = lax.dynamic_slice_in_dim(sky_cube, HALF - HALF * half, HALF, 1)
    for_b = lax.dynamic_slice_in_dim(sky_cube, HALF * half, HALF, 1)
    sky_a, sky_b = pair_swap(for_a, "sky", False), pair_swap(for_b, "sky", True)
    grad, mats, held = back_project(half_width, conv_weight, out_cotangent)
    beam, to_core, to_far = beam_of(mats, sky_cube, sky_b, sky_a, grad)
    from_core, from_far = pair_swap(to_core, "freq", False), pair_swap(to_far, "freq", True)
    inner = inner_terms(beam, held)
    copies = lax.axis_size("freq") * lax.axis_size("sky")
    own, to_a, to_b, terms = spread_and_outer(mats, grad, from_core, from_far, inner, held, copies)
    gathered = lax.all_to_all(terms, ("freq", "sky"), 0, 0)
    row_a, row_b = pair_swap(to_a, "sky", False), pair_swap(to_b, "sky", True)
    cell_count = freq_count * lax.axis_size("freq") * row_count * lax.axis_size("sky") * length
    return finish(1.0 / math.sqrt(cell_count), own, row_a, row_b, gathered)


def solution(mesh):
    return jax.shard_map(
        per_device,
        mesh=mesh,
        in_specs=(P("freq", "sky", None), P("freq"), P(), P(None, "freq", "sky", None)),
        out_specs=(P("freq", "sky", None), P()),
        check_vma=False,
    )
```
